32 devices in a mesh: frow: 4 (over z), fcol: 4 (over x, core), chan: 2 (over y).
Axes of the slice: x: 2, y: 2, z: 4, core: 2. Of those that a mesh axis runs over, the one named last changes fastest.
Arguments:
- image_cube: float32 [32, 256, 1024], P('chan', 'frow', 'fcol'), may hold values from -40 to 40
- weights: float32 [3, 256, 1024], P(None, 'frow', 'fcol'), may hold values from 0.5 to 2
Outputs:
- backprojected: float32 [32, 256, 1024], P('chan', 'frow', 'fcol')
- lowrank: float32 [32, 256, 1024], P('chan', 'frow', 'fcol')
The draws below stay inside these ranges and needn't reach their ends.
All inputs are finite; a program needn't handle non-finite values.
Results may differ from the reference program's by a relative error of at most 0.0003.
Values sent between devices are 32-bit elements; how exact they have to be, the bound alone decides.
A program may use at most 128 MiB of HBM per device.

```python
import math
import jax
import jax.numpy as jnp
import numpy as np
from jax import lax

L = 32
CR = 64
CC = 256
JSWEEPS = 3
NR = 256
NC = 1024
N_FROW = 4
N_FCOL = 4


def draw_image_cube(key, part):
    subkeys = jax.random.split(key, 4)
    noise_part = jax.random.normal(subkeys[0], (L, NR, NC), jnp.float32)
    spectra = 0.7 * jax.random.normal(subkeys[1], (L, 4), jnp.float32)
    sky_maps = jax.random.normal(subkeys[2], (4, NR, NC), jnp.float32)
    rough_part = jax.random.uniform(subkeys[3], (L,), jnp.float32, 0.7, 1.3)
    channel_ramp = 3.0 ** (jnp.arange(L, dtype=jnp.float32) / (L - 1))
    amplitude = channel_ramp * rough_part
    mixture = noise_part + jnp.einsum('lk,kij->lij', spectra, sky_maps)
    return jnp.clip(amplitude[:, None, None] * mixture, -40.0, 40.0).astype(jnp.float32)


def steps_of(stream_key, shape, pieces, smallest, high):
    level, own = 1.0, jax.random.fold_in(stream_key, 6)
    for axis_at, parts in pieces:
        steps = jnp.exp(jax.random.uniform(jax.random.fold_in(own, axis_at), (parts,), jnp.float32, smallest / len(pieces), high / len(pieces)))
        level = level * jnp.repeat(steps, shape[axis_at] // parts).reshape([-1 if axis == axis_at else 1 for axis in range(len(shape))])
    return level


def setup_inputs(seed: int = 0) -> dict:
    arg_keys = jax.random.split(jax.random.key(seed), 3)
    image_cube = draw_image_cube(jax.random.fold_in(arg_keys[2], 71), 0)
    weights = jnp.clip(jnp.exp(math.log(2.0) - 1.3862944 * jax.random.uniform(arg_keys[1], (3, NR, NC), jnp.float32) ** steps_of(arg_keys[1], (3, NR, NC), ((1, 4), (2, 4)), -0.2, 0.2)), 0.5, 2.0)
    return dict(image_cube=image_cube, weights=weights)


filter_taps = (0.0625, 0.25, 0.375, 0.25, 0.0625)
band_levels = (12.0, 4.0, 2.5)
rank_level = 2.0
tiny_value = 1e-30

def smooth(extended, dilation):
    reach_cells = 2 * dilation
    row_count = extended.shape[-2] - 2 * reach_cells
    col_count = extended.shape[-1] - 2 * reach_cells
    across = filter_taps[0] * extended[..., 0:row_count, :]
    for tap_index in range(1, 5):
        offset = tap_index * dilation
        across = across + filter_taps[tap_index] * extended[..., offset:offset + row_count, :]
    result = filter_taps[0] * across[..., 0:col_count]
    for tap_index in range(1, 5):
        offset = tap_index * dilation
        result = result + filter_taps[tap_index] * across[..., offset:offset + col_count]
    return result

def tournament(order_size):
    players = list(range(order_size))
    tables = []
    for round_index in range(order_size - 1):
        first_list = []
        second_list = []
        for slot_index in range(order_size // 2):
            left_one = players[slot_index]
            right_one = players[order_size - 1 - slot_index]
            first_list.append(min(left_one, right_one))
            second_list.append(max(left_one, right_one))
        order_list = np.array(first_list + second_list, np.int32)
        inverse_list = np.argsort(order_list).astype(np.int32)
        tables.append((np.array(first_list, np.int32), np.array(second_list, np.int32), order_list, inverse_list))
        players = [players[0], players[-1]] + players[1:-1]
    return tables

def jacobi(gram_matrix):
    order_size = gram_matrix.shape[0]
    half_size = order_size // 2
    tables = tournament(order_size)
    identity_matrix = jnp.eye(order_size, dtype=gram_matrix.dtype)

    def one_round(matrix, vectors, first_list, second_list, order_list, inverse_list):
        diag_values = jnp.diagonal(matrix)
        left_diag = diag_values[first_list]
        right_diag = diag_values[second_list]
        cross_term = matrix[first_list, second_list]
        gap_value = right_diag - left_diag
        sign_part = jnp.where(gap_value >= 0, 1.0, -1.0)
        tangent = sign_part * 2.0 * cross_term / (jnp.abs(gap_value) + jnp.sqrt(gap_value * gap_value + 4.0 * cross_term * cross_term) + tiny_value)
        cosine = 1.0 / jnp.sqrt(1.0 + tangent * tangent)
        sine_part = tangent * cosine

        def turn_columns(block):
            placed = block[:, order_list]
            left_cols = placed[:, :half_size]
            right_cols = placed[:, half_size:]
            turned = jnp.concatenate([cosine * left_cols - sine_part * right_cols, sine_part * left_cols + cosine * right_cols], axis=1)
            return turned[:, inverse_list]
        matrix = turn_columns(matrix)
        matrix = turn_columns(matrix.T).T
        vectors = turn_columns(vectors)
        return (matrix, vectors)

    def sweep(counter, carried):
        matrix, vectors = carried
        for first_list, second_list, order_list, inverse_list in tables:
            matrix, vectors = one_round(matrix, vectors, first_list, second_list, order_list, inverse_list)
        return (matrix, vectors)
    matrix, vectors = lax.fori_loop(0, JSWEEPS, sweep, (gram_matrix, identity_matrix))
    return (jnp.diagonal(matrix), vectors)

def spectral_map(gram_matrix, threshold):
    values, vectors = jacobi(gram_matrix)
    factors = 1.0 - threshold / jnp.sqrt(jnp.maximum(values, threshold * threshold))
    return jnp.dot(vectors * factors[None, :], vectors.T, precision=lax.Precision.HIGHEST)

def reference(image_cube, weights):
    channels = image_cube.shape[0]
    coarse_one = smooth(jnp.pad(image_cube, ((0, 0), (2, 2), (2, 2))), 1)
    coarse_two = smooth(jnp.pad(coarse_one, ((0, 0), (4, 4), (4, 4))), 2)
    band_list = (image_cube - coarse_one, coarse_one - coarse_two, coarse_two)
    dual_list = []
    for band_index in range(3):
        levels = band_levels[band_index] * weights[band_index]
        totals = lax.optimization_barrier(jnp.sum(band_list[band_index] * band_list[band_index], axis=0))
        dual_list.append(band_list[band_index] * (levels / jnp.sqrt(jnp.maximum(totals, levels * levels))))
    inner_part = smooth(jnp.pad(dual_list[2] - dual_list[1], ((0, 0), (4, 4), (4, 4))), 2)
    summed = dual_list[1] - dual_list[0] + inner_part
    backprojected = dual_list[0] + smooth(jnp.pad(summed, ((0, 0), (2, 2), (2, 2))), 1)
    pixels = CR * CC
    threshold = rank_level * math.sqrt(pixels)
    facets = image_cube.reshape(channels, N_FROW, CR, N_FCOL, CC).transpose(1, 3, 0, 2, 4).reshape(N_FROW * N_FCOL, channels, pixels)

    def project(matrix):
        gram_matrix = jnp.dot(matrix, matrix.T, precision=lax.Precision.HIGHEST)
        mixing = spectral_map(gram_matrix, threshold)
        return jnp.dot(mixing, matrix, precision=lax.Precision.HIGHEST)
    projected = lax.map(project, facets)
    lowrank = projected.reshape(N_FROW, N_FCOL, channels, CR, CC).transpose(2, 0, 3, 1, 4).reshape(channels, N_FROW * CR, N_FCOL * CC)
    return (backprojected, lowrank)
```

```python
import functools
import math

import jax
import jax.numpy as jnp
from jax import lax
from jax.experimental import pallas as pl
from jax.experimental.pallas import tpu as pltpu
from jax.sharding import PartitionSpec as P

JSWEEPS = 3
HALO = 8
REACH = 6
NEAR = 2
PACK = 16
CHUNK = 8
TURNS = 3

filter_taps = (0.0625, 0.25, 0.375, 0.25, 0.0625)
band_levels = (12.0, 4.0, 2.5)
rank_level = 2.0


def down(x, row):
    top, low = x[:8], x[8:]
    a, b = pltpu.roll(top, 1, 0), pltpu.roll(low, 1, 0)
    first = row == 0
    return jnp.concatenate([jnp.where(first, top, a), jnp.where(first, a, b)], axis=0)

def up(x, row):
    top, low = x[:8], x[8:]
    a, b = pltpu.roll(top, 7, 0), pltpu.roll(low, 7, 0)
    final = row == 7
    return jnp.concatenate([jnp.where(final, b, a), jnp.where(final, low, b)], axis=0)

def lanes(x):
    return jnp.broadcast_to(jnp.sum(x, axis=1, keepdims=True), x.shape)

def moved(state, row):
    bt, bl, wt, wl = state
    return [down(v, row) for v in (bt, bl, wt, wl)], [up(v, row) for v in (bt, bl, wt, wl)]

def ahead(moves):
    (bt, bl, _, _), (_, _, wt, wl) = moves
    return lanes(bt * wt), lanes(bt * wl), lanes(bl * wt), lanes(bl * wl)

def rotation(gap, cross, first):
    double = cross + cross
    size = gap * gap + double * double
    flat = size < 1e-36
    inverse = lax.rsqrt(jnp.maximum(size, 1e-36))
    positive = (gap > 0) | ((gap == 0) & first)
    square = jnp.where(flat, 1.0, 0.5 + (0.5 * jnp.abs(gap)) * inverse)
    part = jnp.where(flat, 0.0, jnp.where(positive, cross, -cross) * inverse)
    root = lax.rsqrt(square)
    sine = part * root
    return square * root, sine, sine * root * cross

def rank_round(carry, tie, marks):
    vectors, diag, dots, turn = carry
    row, second, final = marks
    (cosine, sine, shift) = turn
    top, low = diag[0] - shift, diag[1] + shift
    cd, sd, cu, su = down(cosine, row), down(sine, row), up(cosine, row), up(sine, row)
    alpha, beta = jnp.where(second, sd, cd), jnp.where(second, cd, -sd)
    gamma, delta = jnp.where(final, cu, su), jnp.where(final, -su, cu)
    cross = alpha * (gamma * dots[0] + delta * dots[1]) + beta * (gamma * dots[2] + delta * dots[3])
    new_top = jnp.where(second, down(low, row), down(top, row))
    new_low = jnp.where(final, up(top, row), up(low, row))
    turn = rotation(new_low - new_top, cross, tie)
    (dbt, dbl, dwt, dwl), (ubt, ubl, uwt, uwl) = moved(vectors, row)
    vectors = (alpha * dbt + beta * dbl, gamma * ubt + delta * ubl, alpha * dwt + beta * dwl, gamma * uwt + delta * uwl)
    return vectors, (new_top, new_low), ahead(moved(vectors, row)), turn

def first_on_top(index, shape):
    place = lax.broadcasted_iota(jnp.int32, shape, 0)
    cycle = 2 * shape[0] - 1
    top = place - 1 - index
    top = jnp.where(place == 0, -1, jnp.where(top < 0, top + cycle, top))
    low = cycle - 1 - place - index
    low = jnp.where(low < 0, low + cycle, low)
    return top < low


def rank_start(gram, marks):
    row = marks[0]
    half = gram.shape[0] // 2
    shape = (half, gram.shape[1])
    place = lax.broadcasted_iota(jnp.int32, shape, 0)
    lane = lax.broadcasted_iota(jnp.int32, shape, 1)
    flip_row = lax.broadcasted_iota(jnp.int32, (half, half), 0)
    flip_lane = lax.broadcasted_iota(jnp.int32, (half, half), 1)
    flip = jnp.where(flip_row + flip_lane == half - 1, 1.0, 0.0)
    low = jnp.dot(
        flip, gram[half:], precision=lax.Precision.HIGHEST, preferred_element_type=jnp.float32
    )
    sides = (jnp.where(lane == place, 1.0, 0.0), jnp.where(lane == 2 * half - 1 - place, 1.0, 0.0))
    vectors = (gram[:half], low, *sides)
    diag = (lanes(gram[:half] * sides[0]), lanes(low * sides[1]))
    turn = rotation(diag[1] - diag[0], lanes(gram[:half] * sides[1]), first_on_top(0, shape))
    return vectors, diag, ahead(moved(vectors, row)), turn


def rank_finish(carry, threshold):
    vectors, diag = carry[0], carry[1]
    mixing = 0.0
    for side, values in zip(vectors[2:], diag):
        factor = 1.0 - threshold / jnp.sqrt(jnp.maximum(values, threshold * threshold))
        mixing = mixing + lax.dot_general(
            side * factor, side, (((0,), (0,)), ((), ())),
            precision=lax.Precision.HIGHEST, preferred_element_type=jnp.float32,
        )
    return mixing


def split_two(values):
    high = values.astype(jnp.bfloat16)
    low = (values - high.astype(jnp.float32)).astype(jnp.bfloat16)
    return high, low


def tap(offset):
    near = jnp.abs(offset)
    return jnp.where(
        near == 0, filter_taps[2],
        jnp.where(near == 1, filter_taps[3], jnp.where(near == 2, filter_taps[4], 0.0)),
    )


def column_weights(start, total):
    shape = (256, 128)
    source = lax.broadcasted_iota(jnp.int32, shape, 0)
    target = lax.broadcasted_iota(jnp.int32, shape, 1)
    source = jnp.where(source < 192, source, source - 256)
    scale = filter_taps[0]
    one = tap(source - target) * scale
    forward, backward = 0.0, 0.0
    for step in range(-2, 3):
        weight = filter_taps[step + 2] * scale * scale
        between = target + 2 * step
        keep = (between + start >= 0) & (between + start < total)
        forward = forward + jnp.where(keep, weight * tap(source - between), 0.0)
        between = target + step
        keep = (between + start >= 0) & (between + start < total)
        away = source - between
        wide = jnp.where(away % 2 == 0, tap(away // 2), 0.0)
        backward = backward + jnp.where(keep, weight * wide, 0.0)
    return one, forward, backward


def rows_filter(ref, at, count, dilation):
    part = lambda step: ref[pl.ds(at + step * dilation, count)]
    return (part(-2) + part(2)) + 4.0 * (part(-1) + part(1)) + 6.0 * part(0)


def facet_kernel(
    threshold, image_ref, weights_ref, back_ref, rank_ref,
    raw, factors, cube, one_cols, two_cols, middle, coarse, level_rows, sums, other_sums,
    duals, diffs, gram, other_gram, mixing, taps_one, taps_two,
    strips_out, strips_in, corners_in, strips_out_two, strips_in_two, corners_in_two,
    send_sems, recv_sems, local_sems,
):
    channels, rows, cols = image_ref.shape
    wide = cols // 2
    half = rows // 2
    chunks = half // CHUNK
    groups = rows // PACK
    order = 2 * channels
    names = ("frow", "fcol", "chan")
    place = {name: lax.axis_index(name) for name in names}
    count = {name: lax.axis_size(name) for name in names}
    me = place["chan"]
    partner = 1 - me
    mesh_ids = pl.DeviceIdType.MESH
    own = cube.at[me]

    halves = []
    for index, which in enumerate((partner, me)):
        at = pl.ds(pl.multiple_of(which * half, half), half)
        halves.append(pltpu.make_async_copy(
            image_ref.at[:, at], raw.at[:, at], local_sems.at[index]))
        halves[-1].start()
    keep_levels = pltpu.make_async_copy(weights_ref, level_rows, local_sems.at[2])
    keep_levels.start()

    def target(row_step, col_step):
        return (place["frow"] + row_step, place["fcol"] + col_step, me)

    def exists(row_step, col_step):
        found = None
        for name, step in (("frow", row_step), ("fcol", col_step)):
            if step:
                here = place[name] < count[name] - 1 if step > 0 else place[name] > 0
                found = here if found is None else found & here
        return found

    around = [(r, c) for r in (-1, 0, 1) for c in (-1, 0, 1) if (r, c) != (0, 0)]
    has = {key: exists(*key) for key in around}
    mate = (place["frow"], place["fcol"], partner)
    barrier = pltpu.get_barrier_semaphore()
    pl.semaphore_signal(barrier, inc=1, device_id=mate, device_id_type=mesh_ids)
    friends = 1
    for key in around:

        @pl.when(has[key])
        def _(key=key):
            pl.semaphore_signal(barrier, inc=1, device_id=target(*key), device_id_type=mesh_ids)

        friends = friends + jnp.where(has[key], 1, 0)

    def flatten_part(which):
        def body(step, carried):
            at = pl.multiple_of(which * half + step * 8, 8)
            own[pl.ds(HALO + at, 8)] = jnp.swapaxes(raw[:, pl.ds(at, 8), :], 0, 1)
            return carried

        lax.fori_loop(0, half // 8, body, 0)

    halves[0].wait()
    flatten_part(partner)
    pl.semaphore_wait(barrier, friends)

    used = [0]

    def copy_to(source, sink, device):
        index = used[0]
        used[0] += 1
        return pltpu.make_async_remote_copy(
            src_ref=source, dst_ref=sink, send_sem=send_sems.at[index],
            recv_sem=recv_sems.at[index], device_id=device, device_id_type=mesh_ids,
        )

    def cube_parts(owner, which):
        parts = []
        for chunk in range(chunks):
            at = pl.ds(HALO + which * half + chunk * CHUNK, CHUNK)
            parts.append(copy_to(cube.at[owner, at], cube.at[owner, at], mate))
        return parts

    first_parts = cube_parts(me, partner)
    for copy in first_parts:
        copy.start()

    def start_all(copies):
        for goes, _, copy in copies:

            @pl.when(has[goes])
            def _(copy=copy):
                copy.start()

    def arrive_all(copies):
        for _, comes, copy in copies:

            @pl.when(has[comes])
            def _(copy=copy):
                copy.wait_recv()

    def left_all(copies):
        for goes, _, copy in copies:

            @pl.when(has[goes])
            def _(copy=copy):
                copy.wait_send()

    def row_copies(ref, reach):
        top = lambda at: ref.at[pl.ds(at, reach)]
        return [
            ((1, 0), (-1, 0), copy_to(top(HALO + rows - reach), top(HALO - reach), target(1, 0))),
            ((-1, 0), (1, 0), copy_to(top(HALO), top(HALO + rows), target(-1, 0))),
        ]

    def col_copies(out, strips, corners):
        copies = []
        for side, step in ((1, 1), (0, -1)):
            copies.append((
                (0, step), (0, -step),
                copy_to(out.at[side], strips.at[1 - side], target(0, step)),
            ))
            for low, turn in ((0, 1), (1, -1)):
                group = groups - 1 if turn == 1 else 0
                copies.append((
                    (turn, step), (-turn, -step),
                    copy_to(out.at[side, :, group], corners.at[1 - side, low], target(turn, step)),
                ))
        return copies

    lane = lax.broadcasted_iota(jnp.int32, (channels, wide), 1)
    early = lane < 64

    def pack_edges(ref, out, kind):
        def body(group, carried):
            left = right = jnp.zeros((channels, wide), jnp.float32)
            for slot in range(PACK):
                at = HALO + group * PACK + slot
                here = (lane >= slot * 8) & (lane < slot * 8 + 8)
                edge = pltpu.roll(ref[at, :, :wide], slot * 8, 1)
                left = jnp.where(here, edge, left)
                edge = pltpu.roll(ref[at, :, cols - wide :], (slot * 8 + 8) % wide, 1)
                right = jnp.where(here, edge, right)
            out[0, kind, group] = left
            out[1, kind, group] = right
            return carried

        lax.fori_loop(0, groups, body, 0)

    def clear_edges(strips, corners):
        for side, step in ((0, -1), (1, 1)):

            @pl.when(jnp.logical_not(has[(0, step)]))
            def _(side=side):
                strips[side] = jnp.zeros(strips.shape[1:], jnp.float32)

            for low, turn in ((0, -1), (1, 1)):

                @pl.when(jnp.logical_not(has[(turn, step)]))
                def _(side=side, low=low):
                    corners[side, low] = jnp.zeros(corners.shape[2:], jnp.float32)

    def clear_rows(ref, first, last, reach):
        zero = jnp.zeros((reach, channels, cols), jnp.float32)

        @pl.when(jnp.logical_not(has[(-1, 0)]))
        def _():
            ref[pl.ds(first, reach)] = zero

        @pl.when(jnp.logical_not(has[(1, 0)]))
        def _():
            ref[pl.ds(last, reach)] = zero

    halves[1].wait()
    flatten_part(me)
    rows_one = row_copies(own, REACH)
    start_all(rows_one)
    pack_edges(own, strips_out, 0)
    cols_one = col_copies(strips_out, strips_in, corners_in)
    start_all(cols_one)
    clear_rows(own, HALO - REACH, HALO + rows, REACH)
    clear_edges(strips_in, corners_in)
    clear_edges(strips_in_two, corners_in_two)
    for kind, reach in ((0, NEAR), (1, REACH)):
        clear_rows(diffs.at[kind], HALO - reach, HALO + rows, reach)
    gram[...] = jnp.zeros(gram.shape, jnp.float32)

    for side in range(2):
        plain, forward, backward = column_weights(
            place["fcol"] * cols + side * wide, count["fcol"] * cols
        )
        plain, forward, backward = [
            jnp.concatenate([values, values], axis=0).astype(jnp.bfloat16)
            for values in (plain, forward, backward)
        ]
        taps_one[side, :, :wide] = plain
        taps_one[side, :, wide:] = forward
        taps_two[side] = backward

    def doubled(ref, strips, corners, kind, group):
        if group is None:
            line = lambda slot: slot if slot < HALO else slot + rows
            edge = lambda side, slot: (corners[side, 0 if slot < HALO else 1, kind],
                                       (slot + HALO) % PACK)
        else:
            line = lambda slot: HALO + group * PACK + slot
            edge = lambda side, slot: (strips[side, kind, group], slot)
        lefts, rights = [], []
        for slot in range(PACK):
            first, second = ref[line(slot), :, :wide], ref[line(slot), :, wide:]
            before, at = edge(0, slot)
            before = pltpu.roll(before, (wide - 8 - at * 8) % wide, 1)
            after, at = edge(1, slot)
            after = pltpu.roll(after, (wide - at * 8) % wide, 1)
            lefts.append(jnp.concatenate([first, jnp.where(early, second, before)], axis=1))
            rights.append(jnp.concatenate([second, jnp.where(early, after, first)], axis=1))
        return [
            jnp.concatenate(split_two(jnp.concatenate(pieces, axis=0)), axis=1)
            for pieces in (lefts, rights)
        ]

    def store_lines(ref, group, lanes_at, values):
        values = values.reshape(PACK, channels, wide)
        if group is None:
            ref[pl.ds(0, HALO), :, lanes_at] = values[:HALO]
            ref[pl.ds(HALO + rows, HALO), :, lanes_at] = values[HALO:]
        else:
            ref[pl.ds(HALO + group * PACK, PACK), :, lanes_at] = values

    dot = functools.partial(jnp.dot, preferred_element_type=jnp.float32)
    spots = (slice(0, wide), slice(wide, cols))

    def analyse(group):
        for side, values in enumerate(doubled(own, strips_in, corners_in, 0, group)):
            both = dot(values, taps_one[side])
            store_lines(one_cols, group, spots[side], both[:, :wide])
            store_lines(two_cols, group, spots[side], both[:, wide:])

    def each_group(work):
        def body(group, carried):
            work(group)
            return carried

        lax.fori_loop(0, groups, body, 0)
        work(None)

    arrive_all(rows_one)
    arrive_all(cols_one)
    each_group(analyse)

    def smooth_rows(step, carried):
        at = HALO - 4 + step * 8
        middle[pl.ds(at, 8)] = rows_filter(two_cols, at, 8, 1)
        return carried

    lax.fori_loop(0, (rows + 8) // 8, smooth_rows, 0)
    clear_rows(middle, HALO - 4, HALO + rows, 4)

    def collect(step, carried):
        at = pl.multiple_of(step * 8, 8)
        first = rows_filter(one_cols, HALO + at, 8, 1)
        second = rows_filter(middle, HALO + at, 8, 2)
        coarse[0, pl.ds(at, 8)] = first
        coarse[1, pl.ds(at, 8)] = second
        bands = (own[pl.ds(HALO + at, 8)] - first, first - second, second)
        for index, band in enumerate(bands):
            square = band * band
            folded = square[:, :8]
            for start in range(8, channels, 8):
                folded = folded + square[:, start : start + 8]
            sums[index, pl.ds(at, 8)] = jnp.sum(jnp.swapaxes(folded, 0, 1), axis=0)
        return carried

    lax.fori_loop(0, rows // 8, collect, 0)
    share_sums = [copy_to(sums.at[index], other_sums.at[index], mate) for index in range(3)]
    share_sums[0].start()

    block = 4

    def gram_step(step, total):
        at = HALO + me * half + step * block
        sides = [
            jnp.concatenate([cube[side, at + row] for row in range(block)], axis=1)
            for side in range(2)
        ]
        both = jnp.concatenate(split_two(jnp.concatenate(sides, axis=0)), axis=0)
        return total + lax.dot_general(
            both, both, (((1,), (1,)), ((), ())), preferred_element_type=jnp.float32
        )

    product = jnp.zeros((2 * order, 2 * order), jnp.float32)
    for chunk, copy in enumerate(first_parts):
        copy.wait_recv()
        product = lax.fori_loop(
            chunk * CHUNK // block, (chunk + 1) * CHUNK // block, gram_step, product
        )
    gram[:, :order] = (
        product[:order, :order] + (product[:order, order:] + product[order:, :order])
    ) + product[order:, order:]
    share_gram = copy_to(gram, other_gram, mate)
    share_gram.start()
    share_sums[1].start()
    share_sums[2].start()
    second_parts = cube_parts(me, me)
    for copy in second_parts:
        copy.start()

    row = lax.broadcasted_iota(jnp.int32, (8, gram.shape[1]), 0)
    spot = lax.broadcasted_iota(jnp.int32, (channels, gram.shape[1]), 0)
    marks = (row, spot == 1, spot == channels - 1)

    def turns(step, carry):
        for index in range(TURNS):
            at = lax.rem(step * TURNS + index + 1, order - 1)
            carry = rank_round(carry, first_on_top(at, spot.shape), marks)
        return carry

    share_gram.wait_recv()
    state = rank_start(gram[...] + other_gram[...], marks)
    steps = JSWEEPS * (order - 1) // TURNS
    pause = steps // 6
    state = lax.fori_loop(0, pause, turns, state)
    keep_levels.wait()
    for index in range(3):
        share_sums[index].wait_recv()
        levels = band_levels[index] * level_rows[index]
        totals = sums[index] + other_sums[index]
        factors[index] = levels / jnp.sqrt(jnp.maximum(totals, levels * levels))

    def project(step, carried):
        base = pl.multiple_of(step * 8, 8)
        scales = [factors[index, pl.ds(base, 8)] for index in range(3)]
        for line in range(8):
            at = base + line
            first, second = coarse[0, at], coarse[1, at]
            bands = (own[HALO + at] - first, first - second, second)
            dual = [
                band * jnp.broadcast_to(scale[line : line + 1], band.shape)
                for band, scale in zip(bands, scales)
            ]
            duals[at] = dual[0]
            diffs[0, HALO + at] = dual[1] - dual[0]
            diffs[1, HALO + at] = dual[2] - dual[1]
        return carried

    lax.fori_loop(0, rows // 8, project, 0)
    rows_two = row_copies(diffs.at[1], REACH) + row_copies(diffs.at[0], NEAR)
    start_all(rows_two)
    for kind in range(2):
        pack_edges(diffs.at[kind], strips_out_two, kind)
    cols_two = col_copies(strips_out_two, strips_in_two, corners_in_two)
    start_all(cols_two)
    state = lax.fori_loop(pause, steps, turns, state)
    mixing[...] = rank_finish(state, threshold)

    arrive_all(rows_two)
    arrive_all(cols_two)

    def synthesise(group):
        edges = (strips_in_two, corners_in_two)
        for side, values in enumerate(doubled(diffs.at[0], *edges, 0, group)):
            store_lines(one_cols, group, spots[side], dot(values, taps_one[side, :, :wide]))
        for side, values in enumerate(doubled(diffs.at[1], *edges, 1, group)):
            store_lines(two_cols, group, spots[side], dot(values, taps_two[side]))

    each_group(synthesise)

    def gather_rows(step, carried):
        at = HALO - NEAR + step * 4
        middle[pl.ds(at, 4)] = one_cols[pl.ds(at, 4)] + rows_filter(two_cols, at, 4, 2)
        return carried

    lax.fori_loop(0, (rows + 2 * NEAR) // 4, gather_rows, 0)
    clear_rows(middle, HALO - NEAR, HALO + rows, NEAR)

    def deliver(step, carried):
        at = pl.multiple_of(step * 8, 8)
        result = duals[pl.ds(at, 8)] + rows_filter(middle, HALO + at, 8, 1)
        back_ref[:, pl.ds(at, 8), :] = jnp.swapaxes(result, 0, 1)
        return carried

    lax.fori_loop(0, rows // 8, deliver, 0)

    own_rows = pl.ds(pl.multiple_of(me * channels, channels), channels)
    high, low = split_two(mixing[own_rows, :order])
    left = jnp.concatenate([high, high, low, low], axis=1)

    def rank_block(at):
        lines = []
        for line in range(8):
            values = jnp.concatenate(
                [cube[0, HALO + at + line], cube[1, HALO + at + line]], axis=0
            )
            high, low = split_two(values)
            lines.append(dot(left, jnp.concatenate([high, low, high, low], axis=0)))
        result = jnp.concatenate([values[None] for values in lines], axis=0)
        rank_ref[:, pl.ds(at, 8), :] = jnp.swapaxes(result, 0, 1)

    def rank_step(step, carried):
        rank_block(pl.multiple_of(me * half + step * 8, 8))
        return carried

    lax.fori_loop(0, half // 8, rank_step, 0)
    for chunk, copy in enumerate(second_parts):
        copy.wait_recv()
        for step in range(CHUNK // 8):
            rank_block(pl.multiple_of(partner * half + chunk * CHUNK + step * 8, 8))
    for copies in (rows_one, cols_one, rows_two, cols_two):
        left_all(copies)
    for copy in (*first_parts, *second_parts, *share_sums, share_gram):
        copy.wait_send()


def shards(image_cube, weights):
    channels, rows, cols = image_cube.shape
    threshold = rank_level * math.sqrt(rows * cols)
    order = channels * lax.axis_size("chan")
    tall = rows + 2 * HALO
    groups = rows // PACK
    f32 = jnp.float32
    in_hbm = pl.BlockSpec(memory_space=pltpu.HBM)
    in_vmem = pl.BlockSpec(memory_space=pltpu.VMEM)
    vmem = pltpu.VMEM
    lines = (tall, channels, cols)
    copies = 64
    return pl.pallas_call(
        functools.partial(facet_kernel, threshold),
        out_shape=(
            jax.ShapeDtypeStruct(image_cube.shape, f32),
            jax.ShapeDtypeStruct(image_cube.shape, f32),
        ),
        in_specs=[in_hbm, in_hbm],
        out_specs=(in_vmem, in_vmem),
        scratch_shapes=[
            vmem(image_cube.shape, f32),
            vmem((3, rows, cols), f32),
            vmem((2, *lines), f32),
            vmem(lines, f32),
            vmem(lines, f32),
            vmem(lines, f32),
            vmem((2, rows, channels, cols), f32),
            vmem((3, rows, cols), f32),
            vmem((3, rows, cols), f32),
            vmem((3, rows, cols), f32),
            vmem((rows, channels, cols), f32),
            vmem((2, *lines), f32),
            vmem((order, 128), f32),
            vmem((order, 128), f32),
            vmem((128, 128), f32),
            vmem((2, 512, 256), jnp.bfloat16),
            vmem((2, 512, 128), jnp.bfloat16),
            vmem((2, 1, groups, channels, 128), f32),
            vmem((2, 1, groups, channels, 128), f32),
            vmem((2, 2, 1, channels, 128), f32),
            vmem((2, 2, groups, channels, 128), f32),
            vmem((2, 2, groups, channels, 128), f32),
            vmem((2, 2, 2, channels, 128), f32),
            pltpu.SemaphoreType.DMA((copies,)),
            pltpu.SemaphoreType.DMA((copies,)),
            pltpu.SemaphoreType.DMA((3,)),
        ],
        compiler_params=pltpu.CompilerParams(
            collective_id=0, has_side_effects=True, vmem_limit_bytes=50 * 2**20
        ),
    )(image_cube, weights)


def solution(mesh):
    placed = (P("chan", "frow", "fcol"), P(None, "frow", "fcol"))
    return jax.shard_map(
        shards,
        mesh=mesh,
        in_specs=placed,
        out_specs=(P("chan", "frow", "fcol"), P("chan", "frow", "fcol")),
        check_vma=False,
    )
```

```python
import functools
import math

import jax
import jax.numpy as jnp
from jax import lax
from jax.experimental import pallas as pl
from jax.experimental.pallas import tpu as pltpu
from jax.sharding import PartitionSpec as P

JSWEEPS = 3
HALO = 8
REACH = 6
NEAR = 2
PACK = 16
CHUNK = 8
TURNS = 3

filter_taps = (0.0625, 0.25, 0.375, 0.25, 0.0625)
band_levels = (12.0, 4.0, 2.5)
rank_level = 2.0


def down(x, row):
    top, low = x[:8], x[8:]
    a, b = pltpu.roll(top, 1, 0), pltpu.roll(low, 1, 0)
    first = row == 0
    return jnp.concatenate([jnp.where(first, top, a), jnp.where(first, a, b)], axis=0)

def up(x, row):
    top, low = x[:8], x[8:]
    a, b = pltpu.roll(top, 7, 0), pltpu.roll(low, 7, 0)
    final = row == 7
    return jnp.concatenate([jnp.where(final, b, a), jnp.where(final, low, b)], axis=0)

def lanes(x):
    return jnp.broadcast_to(jnp.sum(x, axis=1, keepdims=True), x.shape)

def moved(state, row):
    bt, bl, wt, wl = state
    return [down(v, row) for v in (bt, bl, wt, wl)], [up(v, row) for v in (bt, bl, wt, wl)]

def ahead(moves):
    (bt, bl, _, _), (_, _, wt, wl) = moves
    return lanes(bt * wt), lanes(bt * wl), lanes(bl * wt), lanes(bl * wl)

def rotation(gap, cross, first):
    double = cross + cross
    size = gap * gap + double * double
    flat = size < 1e-36
    inverse = lax.rsqrt(jnp.maximum(size, 1e-36))
    positive = (gap > 0) | ((gap == 0) & first)
    square = jnp.where(flat, 1.0, 0.5 + (0.5 * jnp.abs(gap)) * inverse)
    part = jnp.where(flat, 0.0, jnp.where(positive, cross, -cross) * inverse)
    root = lax.rsqrt(square)
    sine = part * root
    return square * root, sine, sine * root * cross

def rank_round(carry, tie, marks):
    vectors, diag, dots, turn = carry
    row, second, final = marks
    (cosine, sine, shift) = turn
    top, low = diag[0] - shift, diag[1] + shift
    cd, sd, cu, su = down(cosine, row), down(sine, row), up(cosine, row), up(sine, row)
    alpha, beta = jnp.where(second, sd, cd), jnp.where(second, cd, -sd)
    gamma, delta = jnp.where(final, cu, su), jnp.where(final, -su, cu)
    cross = alpha * (gamma * dots[0] + delta * dots[1]) + beta * (gamma * dots[2] + delta * dots[3])
    new_top = jnp.where(second, down(low, row), down(top, row))
    new_low = jnp.where(final, up(top, row), up(low, row))
    turn = rotation(new_low - new_top, cross, tie)
    (dbt, dbl, dwt, dwl), (ubt, ubl, uwt, uwl) = moved(vectors, row)
    vectors = (alpha * dbt + beta * dbl, gamma * ubt + delta * ubl, alpha * dwt + beta * dwl, gamma * uwt + delta * uwl)
    return vectors, (new_top, new_low), ahead(moved(vectors, row)), turn

def first_on_top(index, shape):
    place = lax.broadcasted_iota(jnp.int32, shape, 0)
    cycle = 2 * shape[0] - 1
    top = place - 1 - index
    top = jnp.where(place == 0, -1, jnp.where(top < 0, top + cycle, top))
    low = cycle - 1 - place - index
    low = jnp.where(low < 0, low + cycle, low)
    return top < low


def rank_start(gram, marks):
    row = marks[0]
    half = gram.shape[0] // 2
    shape = (half, gram.shape[1])
    place = lax.broadcasted_iota(jnp.int32, shape, 0)
    lane = lax.broadcasted_iota(jnp.int32, shape, 1)
    flip_row = lax.broadcasted_iota(jnp.int32, (half, half), 0)
    flip_lane = lax.broadcasted_iota(jnp.int32, (half, half), 1)
    flip = jnp.where(flip_row + flip_lane == half - 1, 1.0, 0.0)
    low = jnp.dot(
        flip, gram[half:], precision=lax.Precision.HIGHEST, preferred_element_type=jnp.float32
    )
    sides = (jnp.where(lane == place, 1.0, 0.0), jnp.where(lane == 2 * half - 1 - place, 1.0, 0.0))
    vectors = (gram[:half], low, *sides)
    diag = (lanes(gram[:half] * sides[0]), lanes(low * sides[1]))
    turn = rotation(diag[1] - diag[0], lanes(gram[:half] * sides[1]), first_on_top(0, shape))
    return vectors, diag, ahead(moved(vectors, row)), turn


def rank_finish(carry, threshold):
    vectors, diag = carry[0], carry[1]
    mixing = 0.0
    for side, values in zip(vectors[2:], diag):
        factor = 1.0 - threshold / jnp.sqrt(jnp.maximum(values, threshold * threshold))
        mixing = mixing + lax.dot_general(
            side * factor, side, (((0,), (0,)), ((), ())),
            precision=lax.Precision.HIGHEST, preferred_element_type=jnp.float32,
        )
    return mixing


def split_two(values):
    high = values.astype(jnp.bfloat16)
    low = (values - high.astype(jnp.float32)).astype(jnp.bfloat16)
    return high, low


def tap(offset):
    near = jnp.abs(offset)
    return jnp.where(
        near == 0, filter_taps[2],
        jnp.where(near == 1, filter_taps[3], jnp.where(near == 2, filter_taps[4], 0.0)),
    )


def column_weights(start, total):
    shape = (256, 128)
    source = lax.broadcasted_iota(jnp.int32, shape, 0)
    target = lax.broadcasted_iota(jnp.int32, shape, 1)
    source = jnp.where(source < 192, source, source - 256)
    scale = filter_taps[0]
    one = tap(source - target) * scale
    forward, backward = 0.0, 0.0
    for step in range(-2, 3):
        weight = filter_taps[step + 2] * scale * scale
        between = target + 2 * step
        keep = (between + start >= 0) & (between + start < total)
        forward = forward + jnp.where(keep, weight * tap(source - between), 0.0)
        between = target + step
        keep = (between + start >= 0) & (between + start < total)
        away = source - between
        wide = jnp.where(away % 2 == 0, tap(away // 2), 0.0)
        backward = backward + jnp.where(keep, weight * wide, 0.0)
    return one, forward, backward


def rows_filter(ref, at, count, dilation):
    part = lambda step: ref[pl.ds(at + step * dilation, count)]
    return (part(-2) + part(2)) + 4.0 * (part(-1) + part(1)) + 6.0 * part(0)


def facet_kernel(
    threshold, image_ref, weights_ref, back_ref, rank_ref,
    raw, factors, cube, one_cols, two_cols, middle, coarse, level_rows, sums, other_sums,
    duals, diffs, gram, other_gram, mixing, taps_one, taps_two,
    strips_out, strips_in, corners_in, strips_out_two, strips_in_two, corners_in_two,
    send_sems, recv_sems, local_sems,
):
    channels, rows, cols = image_ref.shape
    wide = cols // 2
    half = rows // 2
    chunks = half // CHUNK
    groups = rows // PACK
    order = 2 * channels
    names = ("frow", "fcol", "chan")
    place = {name: lax.axis_index(name) for name in names}
    count = {name: lax.axis_size(name) for name in names}
    me = place["chan"]
    partner = 1 - me
    mesh_ids = pl.DeviceIdType.MESH
    own = cube.at[me]

    halves = []
    for index, which in enumerate((partner, me)):
        at = pl.ds(pl.multiple_of(which * half, half), half)
        halves.append(pltpu.make_async_copy(
            image_ref.at[:, at], raw.at[:, at], local_sems.at[index]))
        halves[-1].start()
    keep_levels = pltpu.make_async_copy(weights_ref, level_rows, local_sems.at[2])
    keep_levels.start()

    def target(row_step, col_step):
        return (place["frow"] + row_step, place["fcol"] + col_step, me)

    def exists(row_step, col_step):
        found = None
        for name, step in (("frow", row_step), ("fcol", col_step)):
            if step:
                here = place[name] < count[name] - 1 if step > 0 else place[name] > 0
                found = here if found is None else found & here
        return found

    around = [(r, c) for r in (-1, 0, 1) for c in (-1, 0, 1) if (r, c) != (0, 0)]
    has = {key: exists(*key) for key in around}
    mate = (place["frow"], place["fcol"], partner)
    barrier = pltpu.get_barrier_semaphore()
    pl.semaphore_signal(barrier, inc=1, device_id=mate, device_id_type=mesh_ids)
    friends = 1
    for key in around:

        @pl.when(has[key])
        def _(key=key):
            pl.semaphore_signal(barrier, inc=1, device_id=target(*key), device_id_type=mesh_ids)

        friends = friends + jnp.where(has[key], 1, 0)

    def flatten_part(which):
        def body(step, carried):
            at = pl.multiple_of(which * half + step * 8, 8)
            own[pl.ds(HALO + at, 8)] = jnp.swapaxes(raw[:, pl.ds(at, 8), :], 0, 1)
            return carried

        lax.fori_loop(0, half // 8, body, 0)

    halves[0].wait()
    flatten_part(partner)
    pl.semaphore_wait(barrier, friends)

    used = [0]

    def copy_to(source, sink, device):
        index = used[0]
        used[0] += 1
        return pltpu.make_async_remote_copy(
            src_ref=source, dst_ref=sink, send_sem=send_sems.at[index],
            recv_sem=recv_sems.at[index], device_id=device, device_id_type=mesh_ids,
        )

    def cube_parts(owner, which):
        parts = []
        for chunk in range(chunks):
            at = pl.ds(HALO + which * half + chunk * CHUNK, CHUNK)
            parts.append(copy_to(cube.at[owner, at], cube.at[owner, at], mate))
        return parts

    first_parts = cube_parts(me, partner)
    for copy in first_parts:
        copy.start()

    def start_all(copies):
        for goes, _, copy in copies:

            @pl.when(has[goes])
            def _(copy=copy):
                copy.start()

    def arrive_all(copies):
        for _, comes, copy in copies:

            @pl.when(has[comes])
            def _(copy=copy):
                copy.wait_recv()

    def left_all(copies):
        for goes, _, copy in copies:

            @pl.when(has[goes])
            def _(copy=copy):
                copy.wait_send()

    def row_copies(ref, reach):
        top = lambda at: ref.at[pl.ds(at, reach)]
        return [
            ((1, 0), (-1, 0), copy_to(top(HALO + rows - reach), top(HALO - reach), target(1, 0))),
            ((-1, 0), (1, 0), copy_to(top(HALO), top(HALO + rows), target(-1, 0))),
        ]

    def col_copies(out, strips, corners):
        copies = []
        for side, step in ((1, 1), (0, -1)):
            copies.append((
                (0, step), (0, -step),
                copy_to(out.at[side], strips.at[1 - side], target(0, step)),
            ))
            for low, turn in ((0, 1), (1, -1)):
                group = groups - 1 if turn == 1 else 0
                copies.append((
                    (turn, step), (-turn, -step),
                    copy_to(out.at[side, :, group], corners.at[1 - side, low], target(turn, step)),
                ))
        return copies

    lane = lax.broadcasted_iota(jnp.int32, (channels, wide), 1)
    early = lane < 64

    def pack_edges(ref, out, kind):
        def body(group, carried):
            left = right = jnp.zeros((channels, wide), jnp.float32)
            for slot in range(PACK):
                at = HALO + group * PACK + slot
                here = (lane >= slot * 8) & (lane < slot * 8 + 8)
                edge = pltpu.roll(ref[at, :, :wide], slot * 8, 1)
                left = jnp.where(here, edge, left)
                edge = pltpu.roll(ref[at, :, cols - wide :], (slot * 8 + 8) % wide, 1)
                right = jnp.where(here, edge, right)
            out[0, kind, group] = left
            out[1, kind, group] = right
            return carried

        lax.fori_loop(0, groups, body, 0)

    def clear_edges(strips, corners):
        for side, step in ((0, -1), (1, 1)):

            @pl.when(jnp.logical_not(has[(0, step)]))
            def _(side=side):
                strips[side] = jnp.zeros(strips.shape[1:], jnp.float32)

            for low, turn in ((0, -1), (1, 1)):

                @pl.when(jnp.logical_not(has[(turn, step)]))
                def _(side=side, low=low):
                    corners[side, low] = jnp.zeros(corners.shape[2:], jnp.float32)

    def clear_rows(ref, first, last, reach):
        zero = jnp.zeros((reach, channels, cols), jnp.float32)

        @pl.when(jnp.logical_not(has[(-1, 0)]))
        def _():
            ref[pl.ds(first, reach)] = zero

        @pl.when(jnp.logical_not(has[(1, 0)]))
        def _():
            ref[pl.ds(last, reach)] = zero

    halves[1].wait()
    flatten_part(me)
    rows_one = row_copies(own, REACH)
    start_all(rows_one)
    pack_edges(own, strips_out, 0)
    cols_one = col_copies(strips_out, strips_in, corners_in)
    start_all(cols_one)
    clear_rows(own, HALO - REACH, HALO + rows, REACH)
    clear_edges(strips_in, corners_in)
    clear_edges(strips_in_two, corners_in_two)
    for kind, reach in ((0, NEAR), (1, REACH)):
        clear_rows(diffs.at[kind], HALO - reach, HALO + rows, reach)
    gram[...] = jnp.zeros(gram.shape, jnp.float32)

    for side in range(2):
        plain, forward, backward = column_weights(
            place["fcol"] * cols + side * wide, count["fcol"] * cols
        )
        plain, forward, backward = [
            jnp.concatenate([values, values], axis=0).astype(jnp.bfloat16)
            for values in (plain, forward, backward)
        ]
        taps_one[side, :, :wide] = plain
        taps_one[side, :, wide:] = forward
        taps_two[side] = backward

    def doubled(ref, strips, corners, kind, group):
        if group is None:
            line = lambda slot: slot if slot < HALO else slot + rows
            edge = lambda side, slot: (corners[side, 0 if slot < HALO else 1, kind],
                                       (slot + HALO) % PACK)
        else:
            line = lambda slot: HALO + group * PACK + slot
            edge = lambda side, slot: (strips[side, kind, group], slot)
        lefts, rights = [], []
        for slot in range(PACK):
            first, second = ref[line(slot), :, :wide], ref[line(slot), :, wide:]
            before, at = edge(0, slot)
            before = pltpu.roll(before, (wide - 8 - at * 8) % wide, 1)
            after, at = edge(1, slot)
            after = pltpu.roll(after, (wide - at * 8) % wide, 1)
            lefts.append(jnp.concatenate([first, jnp.where(early, second, before)], axis=1))
            rights.append(jnp.concatenate([second, jnp.where(early, after, first)], axis=1))
        return [
            jnp.concatenate(split_two(jnp.concatenate(pieces, axis=0)), axis=1)
            for pieces in (lefts, rights)
        ]

    def store_lines(ref, group, lanes_at, values):
        values = values.reshape(PACK, channels, wide)
        if group is None:
            ref[pl.ds(0, HALO), :, lanes_at] = values[:HALO]
            ref[pl.ds(HALO + rows, HALO), :, lanes_at] = values[HALO:]
        else:
            ref[pl.ds(HALO + group * PACK, PACK), :, lanes_at] = values

    dot = functools.partial(jnp.dot, preferred_element_type=jnp.float32)
    spots = (slice(0, wide), slice(wide, cols))

    def analyse(group):
        for side, values in enumerate(doubled(own, strips_in, corners_in, 0, group)):
            both = dot(values, taps_one[side])
            store_lines(one_cols, group, spots[side], both[:, :wide])
            store_lines(two_cols, group, spots[side], both[:, wide:])

    def each_group(work):
        def body(group, carried):
            work(group)
            return carried

        lax.fori_loop(0, groups, body, 0)
        work(None)

    arrive_all(rows_one)
    arrive_all(cols_one)
    each_group(analyse)

    def smooth_rows(step, carried):
        at = HALO - 4 + step * 8
        middle[pl.ds(at, 8)] = rows_filter(two_cols, at, 8, 1)
        return carried

    lax.fori_loop(0, (rows + 8) // 8, smooth_rows, 0)
    clear_rows(middle, HALO - 4, HALO + rows, 4)

    def collect(step, carried):
        at = pl.multiple_of(step * 8, 8)
        first = rows_filter(one_cols, HALO + at, 8, 1)
        second = rows_filter(middle, HALO + at, 8, 2)
        coarse[0, pl.ds(at, 8)] = first
        coarse[1, pl.ds(at, 8)] = second
        bands = (own[pl.ds(HALO + at, 8)] - first, first - second, second)
        for index, band in enumerate(bands):
            square = band * band
            folded = square[:, :8]
            for start in range(8, channels, 8):
                folded = folded + square[:, start : start + 8]
            sums[index, pl.ds(at, 8)] = jnp.sum(jnp.swapaxes(folded, 0, 1), axis=0)
        return carried

    lax.fori_loop(0, rows // 8, collect, 0)
    share_sums = [copy_to(sums.at[index], other_sums.at[index], mate) for index in range(3)]
    share_sums[0].start()

    block = 4

    def gram_step(step, total):
        at = HALO + me * half + step * block
        sides = [
            jnp.concatenate([cube[side, at + row] for row in range(block)], axis=1)
            for side in range(2)
        ]
        both = jnp.concatenate(split_two(jnp.concatenate(sides, axis=0)), axis=0)
        return total + lax.dot_general(
            both, both, (((1,), (1,)), ((), ())), preferred_element_type=jnp.float32
        )

    product = jnp.zeros((2 * order, 2 * order), jnp.float32)
    for chunk, copy in enumerate(first_parts):
        copy.wait_recv()
        product = lax.fori_loop(
            chunk * CHUNK // block, (chunk + 1) * CHUNK // block, gram_step, product
        )
    gram[:, :order] = (
        product[:order, :order] + (product[:order, order:] + product[order:, :order])
    ) + product[order:, order:]
    share_gram = copy_to(gram, other_gram, mate)
    share_gram.start()
    share_sums[1].start()
    share_sums[2].start()
    second_parts = cube_parts(me, me)
    for copy in second_parts:
        copy.start()

    row = lax.broadcasted_iota(jnp.int32, (8, gram.shape[1]), 0)
    spot = lax.broadcasted_iota(jnp.int32, (channels, gram.shape[1]), 0)
    marks = (row, spot == 1, spot == channels - 1)

    def turns(step, carry):
        for index in range(TURNS):
            at = lax.rem(step * TURNS + index + 1, order - 1)
            carry = rank_round(carry, first_on_top(at, spot.shape), marks)
        return carry

    share_gram.wait_recv()
    state = rank_start(gram[...] + other_gram[...], marks)
    steps = JSWEEPS * (order - 1) // TURNS
    pause = steps // 6
    state = lax.fori_loop(0, pause, turns, state)
    keep_levels.wait()
    for index in range(3):
        share_sums[index].wait_recv()
        levels = band_levels[index] * level_rows[index]
        totals = sums[index] + other_sums[index]
        factors[index] = levels / jnp.sqrt(jnp.maximum(totals, levels * levels))

    def project(step, carried):
        base = pl.multiple_of(step * 8, 8)
        scales = [factors[index, pl.ds(base, 8)] for index in range(3)]
        for line in range(8):
            at = base + line
            first, second = coarse[0, at], coarse[1, at]
            bands = (own[HALO + at] - first, first - second, second)
            dual = [
                band * jnp.broadcast_to(scale[line : line + 1], band.shape)
                for band, scale in zip(bands, scales)
            ]
            duals[at] = dual[0]
            diffs[0, HALO + at] = dual[1] - dual[0]
            diffs[1, HALO + at] = dual[2] - dual[1]
        return carried

    lax.fori_loop(0, rows // 8, project, 0)
    rows_two = row_copies(diffs.at[1], REACH) + row_copies(diffs.at[0], NEAR)
    start_all(rows_two)
    for kind in range(2):
        pack_edges(diffs.at[kind], strips_out_two, kind)
    cols_two = col_copies(strips_out_two, strips_in_two, corners_in_two)
    start_all(cols_two)
    state = lax.fori_loop(pause, steps, turns, state)
    mixing[...] = rank_finish(state, threshold)

    arrive_all(rows_two)
    arrive_all(cols_two)

    def synthesise(group):
        edges = (strips_in_two, corners_in_two)
        for side, values in enumerate(doubled(diffs.at[0], *edges, 0, group)):
            store_lines(one_cols, group, spots[side], dot(values, taps_one[side, :, :wide]))
        for side, values in enumerate(doubled(diffs.at[1], *edges, 1, group)):
            store_lines(two_cols, group, spots[side], dot(values, taps_two[side]))

    each_group(synthesise)

    def gather_rows(step, carried):
        at = HALO - NEAR + step * 4
        middle[pl.ds(at, 4)] = one_cols[pl.ds(at, 4)] + rows_filter(two_cols, at, 4, 2)
        return carried

    lax.fori_loop(0, (rows + 2 * NEAR) // 4, gather_rows, 0)
    clear_rows(middle, HALO - NEAR, HALO + rows, NEAR)

    def deliver(step, carried):
        at = pl.multiple_of(step * 8, 8)
        result = duals[pl.ds(at, 8)] + rows_filter(middle, HALO + at, 8, 1)
        back_ref[:, pl.ds(at, 8), :] = jnp.swapaxes(result, 0, 1)
        return carried

    lax.fori_loop(0, rows // 8, deliver, 0)

    own_rows = pl.ds(pl.multiple_of(me * channels, channels), channels)
    high, low = split_two(mixing[own_rows, :order])
    left = jnp.concatenate([high, high, low, low], axis=1)

    def rank_block(at):
        lines = []
        for line in range(8):
            values = jnp.concatenate(
                [cube[0, HALO + at + line], cube[1, HALO + at + line]], axis=0
            )
            high, low = split_two(values)
            lines.append(dot(left, jnp.concatenate([high, low, high, low], axis=0)))
        result = jnp.concatenate([values[None] for values in lines], axis=0)
        rank_ref[:, pl.ds(at, 8), :] = jnp.swapaxes(result, 0, 1)

    def rank_step(step, carried):
        rank_block(pl.multiple_of(me * half + step * 8, 8))
        return carried

    lax.fori_loop(0, half // 8, rank_step, 0)
    for chunk, copy in enumerate(second_parts):
        copy.wait_recv()
        for step in range(CHUNK // 8):
            rank_block(pl.multiple_of(partner * half + chunk * CHUNK + step * 8, 8))
    for copies in (rows_one, cols_one, rows_two, cols_two):
        left_all(copies)
    for copy in (*first_parts, *second_parts, *share_sums, share_gram):
        copy.wait_send()


def shards(image_cube, weights):
    channels, rows, cols = image_cube.shape
    threshold = rank_level * math.sqrt(rows * cols)
    order = channels * lax.axis_size("chan")
    tall = rows + 2 * HALO
    groups = rows // PACK
    f32 = jnp.float32
    in_hbm = pl.BlockSpec(memory_space=pltpu.HBM)
    in_vmem = pl.BlockSpec(memory_space=pltpu.VMEM)
    vmem = pltpu.VMEM
    lines = (tall, channels, cols)
    copies = 64
    stay = lambda array: pltpu.with_memory_space_constraint(array, pltpu.HBM)
    return pl.pallas_call(
        functools.partial(facet_kernel, threshold),
        out_shape=(
            jax.ShapeDtypeStruct(image_cube.shape, f32),
            jax.ShapeDtypeStruct(image_cube.shape, f32),
        ),
        in_specs=[in_hbm, in_hbm],
        out_specs=(in_vmem, in_vmem),
        scratch_shapes=[
            vmem(image_cube.shape, f32),
            vmem((3, rows, cols), f32),
            vmem((2, *lines), f32),
            vmem(lines, f32),
            vmem(lines, f32),
            vmem(lines, f32),
            vmem((2, rows, channels, cols), f32),
            vmem((3, rows, cols), f32),
            vmem((3, rows, cols), f32),
            vmem((3, rows, cols), f32),
            vmem((rows, channels, cols), f32),
            vmem((2, *lines), f32),
            vmem((order, 128), f32),
            vmem((order, 128), f32),
            vmem((128, 128), f32),
            vmem((2, 512, 256), jnp.bfloat16),
            vmem((2, 512, 128), jnp.bfloat16),
            vmem((2, 1, groups, channels, 128), f32),
            vmem((2, 1, groups, channels, 128), f32),
            vmem((2, 2, 1, channels, 128), f32),
            vmem((2, 2, groups, channels, 128), f32),
            vmem((2, 2, groups, channels, 128), f32),
            vmem((2, 2, 2, channels, 128), f32),
            pltpu.SemaphoreType.DMA((copies,)),
            pltpu.SemaphoreType.DMA((copies,)),
            pltpu.SemaphoreType.DMA((3,)),
        ],
        compiler_params=pltpu.CompilerParams(
            collective_id=0, has_side_effects=True, vmem_limit_bytes=50 * 2**20
        ),
    )(stay(image_cube), stay(weights))


def solution(mesh):
    placed = (P("chan", "frow", "fcol"), P(None, "frow", "fcol"))
    return jax.shard_map(
        shards,
        mesh=mesh,
        in_specs=placed,
        out_specs=(P("chan", "frow", "fcol"), P("chan", "frow", "fcol")),
        check_vma=False,
    )
```

```python
import functools
import math

import jax
import jax.numpy as jnp
from jax import lax
from jax.experimental import pallas as pl
from jax.experimental.pallas import tpu as pltpu
from jax.sharding import PartitionSpec as P

JSWEEPS = 3
HALO = 8
REACH = 6
NEAR = 2
PACK = 16
CHUNK = 8
TURNS = 16
PIECES = 4

filter_taps = (0.0625, 0.25, 0.375, 0.25, 0.0625)
band_levels = (12.0, 4.0, 2.5)
rank_level = 2.0


def down(x, row):
    top, low = x[:8], x[8:]
    a, b = pltpu.roll(top, 1, 0), pltpu.roll(low, 1, 0)
    first = row == 0
    return jnp.concatenate([jnp.where(first, top, a), jnp.where(first, a, b)], axis=0)

def up(x, row):
    top, low = x[:8], x[8:]
    a, b = pltpu.roll(top, 7, 0), pltpu.roll(low, 7, 0)
    final = row == 7
    return jnp.concatenate([jnp.where(final, b, a), jnp.where(final, low, b)], axis=0)

def lanes(x):
    return jnp.broadcast_to(jnp.sum(x, axis=1, keepdims=True), x.shape)

def moved(state, row):
    bt, bl, wt, wl = state
    return [down(v, row) for v in (bt, bl, wt, wl)], [up(v, row) for v in (bt, bl, wt, wl)]

def ahead(moves):
    (bt, bl, _, _), (_, _, wt, wl) = moves
    return lanes(bt * wt), lanes(bt * wl), lanes(bl * wt), lanes(bl * wl)

def rotation(gap, cross, first):
    double = cross + cross
    size = gap * gap + double * double
    flat = size < 1e-36
    inverse = lax.rsqrt(jnp.maximum(size, 1e-36))
    positive = (gap > 0) | ((gap == 0) & first)
    square = jnp.where(flat, 1.0, 0.5 + (0.5 * jnp.abs(gap)) * inverse)
    part = jnp.where(flat, 0.0, jnp.where(positive, cross, -cross) * inverse)
    root = lax.rsqrt(square)
    sine = part * root
    return square * root, sine, sine * root * cross

def rank_round(carry, tie, marks):
    vectors, diag, dots, turn = carry
    row, second, final = marks
    (cosine, sine, shift) = turn
    top, low = diag[0] - shift, diag[1] + shift
    cd, sd, cu, su = down(cosine, row), down(sine, row), up(cosine, row), up(sine, row)
    alpha, beta = jnp.where(second, sd, cd), jnp.where(second, cd, -sd)
    gamma, delta = jnp.where(final, cu, su), jnp.where(final, -su, cu)
    cross = alpha * (gamma * dots[0] + delta * dots[1]) + beta * (gamma * dots[2] + delta * dots[3])
    new_top = jnp.where(second, down(low, row), down(top, row))
    new_low = jnp.where(final, up(top, row), up(low, row))
    turn = rotation(new_low - new_top, cross, tie)
    (dbt, dbl, dwt, dwl), (ubt, ubl, uwt, uwl) = moved(vectors, row)
    vectors = (alpha * dbt + beta * dbl, gamma * ubt + delta * ubl, alpha * dwt + beta * dwl, gamma * uwt + delta * uwl)
    return vectors, (new_top, new_low), ahead(moved(vectors, row)), turn

def first_on_top(index, shape):
    place = lax.broadcasted_iota(jnp.int32, shape, 0)
    cycle = 2 * shape[0] - 1
    top = place - 1 - index
    top = jnp.where(place == 0, -1, jnp.where(top < 0, top + cycle, top))
    low = cycle - 1 - place - index
    low = jnp.where(low < 0, low + cycle, low)
    return top < low


def rank_start(gram, marks):
    row = marks[0]
    half = gram.shape[0] // 2
    shape = (half, gram.shape[1])
    place = lax.broadcasted_iota(jnp.int32, shape, 0)
    lane = lax.broadcasted_iota(jnp.int32, shape, 1)
    flip_row = lax.broadcasted_iota(jnp.int32, (half, half), 0)
    flip_lane = lax.broadcasted_iota(jnp.int32, (half, half), 1)
    flip = jnp.where(flip_row + flip_lane == half - 1, 1.0, 0.0)
    low = jnp.dot(
        flip, gram[half:], precision=lax.Precision.HIGHEST, preferred_element_type=jnp.float32
    )
    sides = (jnp.where(lane == place, 1.0, 0.0), jnp.where(lane == 2 * half - 1 - place, 1.0, 0.0))
    vectors = (gram[:half], low, *sides)
    diag = (lanes(gram[:half] * sides[0]), lanes(low * sides[1]))
    turn = rotation(diag[1] - diag[0], lanes(gram[:half] * sides[1]), first_on_top(0, shape))
    return vectors, diag, ahead(moved(vectors, row)), turn


def rank_finish(carry, threshold):
    vectors, diag = carry[0], carry[1]
    mixing = 0.0
    for side, values in zip(vectors[2:], diag):
        factor = 1.0 - threshold / jnp.sqrt(jnp.maximum(values, threshold * threshold))
        mixing = mixing + lax.dot_general(
            side * factor, side, (((0,), (0,)), ((), ())),
            precision=lax.Precision.HIGHEST, preferred_element_type=jnp.float32,
        )
    return mixing


def split_two(values):
    high = values.astype(jnp.bfloat16)
    low = (values - high.astype(jnp.float32)).astype(jnp.bfloat16)
    return high, low


def tap(offset):
    near = jnp.abs(offset)
    return jnp.where(
        near == 0, filter_taps[2],
        jnp.where(near == 1, filter_taps[3], jnp.where(near == 2, filter_taps[4], 0.0)),
    )


def column_weights(start, total):
    shape = (256, 128)
    source = lax.broadcasted_iota(jnp.int32, shape, 0)
    target = lax.broadcasted_iota(jnp.int32, shape, 1)
    source = jnp.where(source < 192, source, source - 256)
    scale = filter_taps[0]
    one = tap(source - target) * scale
    forward, backward = 0.0, 0.0
    for step in range(-2, 3):
        weight = filter_taps[step + 2] * scale * scale
        between = target + 2 * step
        keep = (between + start >= 0) & (between + start < total)
        forward = forward + jnp.where(keep, weight * tap(source - between), 0.0)
        between = target + step
        keep = (between + start >= 0) & (between + start < total)
        away = source - between
        wide = jnp.where(away % 2 == 0, tap(away // 2), 0.0)
        backward = backward + jnp.where(keep, weight * wide, 0.0)
    return one, forward, backward


def rows_filter(ref, at, count, dilation):
    part = lambda step: ref[pl.ds(at + step * dilation, count)]
    return (part(-2) + part(2)) + 4.0 * (part(-1) + part(1)) + 6.0 * part(0)


def facet_kernel(
    threshold, image_ref, weights_ref, back_ref, rank_ref,
    raw, factors, cube, one_cols, two_cols, middle, coarse, level_rows, sums, other_sums,
    duals, diffs, gram, other_gram, mixing, taps_one, taps_two,
    strips_out, strips_in, corners_in, strips_out_two, strips_in_two, corners_in_two,
    send_sems, recv_sems, local_sems,
):
    channels, rows, cols = image_ref.shape
    wide = cols // 2
    half = rows // 2
    chunks = half // CHUNK
    groups = rows // PACK
    order = 2 * channels
    names = ("frow", "fcol", "chan")
    place = {name: lax.axis_index(name) for name in names}
    count = {name: lax.axis_size(name) for name in names}
    me = place["chan"]
    partner = 1 - me
    mesh_ids = pl.DeviceIdType.MESH
    own = cube.at[me]

    loads = []
    for chunk in range(chunks + 1):
        if chunk < chunks:
            at = pl.ds(pl.multiple_of(partner * half + chunk * CHUNK, CHUNK), CHUNK)
        else:
            at = pl.ds(pl.multiple_of(me * half, half), half)
        loads.append(pltpu.make_async_copy(
            image_ref.at[:, at], raw.at[:, at], local_sems.at[chunk]))
        loads[-1].start()
    keep_levels = pltpu.make_async_copy(weights_ref, level_rows, local_sems.at[chunks + 1])
    keep_levels.start()

    def target(row_step, col_step):
        return (place["frow"] + row_step, place["fcol"] + col_step, me)

    def exists(row_step, col_step):
        found = None
        for name, step in (("frow", row_step), ("fcol", col_step)):
            if step:
                here = place[name] < count[name] - 1 if step > 0 else place[name] > 0
                found = here if found is None else found & here
        return found

    around = [(r, c) for r in (-1, 0, 1) for c in (-1, 0, 1) if (r, c) != (0, 0)]
    has = {key: exists(*key) for key in around}
    mate = (place["frow"], place["fcol"], partner)
    barrier = pltpu.get_barrier_semaphore()
    pl.semaphore_signal(barrier, inc=1, device_id=mate, device_id_type=mesh_ids)
    friends = 1
    for key in around:

        @pl.when(has[key])
        def _(key=key):
            pl.semaphore_signal(barrier, inc=1, device_id=target(*key), device_id_type=mesh_ids)

        friends = friends + jnp.where(has[key], 1, 0)

    def flatten_part(start, size):
        def body(step, carried):
            at = pl.multiple_of(start + step * 8, 8)
            own[pl.ds(HALO + at, 8)] = jnp.swapaxes(raw[:, pl.ds(at, 8), :], 0, 1)
            return carried

        lax.fori_loop(0, size // 8, body, 0)

    used = [0]

    def copy_to(source, sink, device):
        index = used[0]
        used[0] += 1
        return pltpu.make_async_remote_copy(
            src_ref=source, dst_ref=sink, send_sem=send_sems.at[index],
            recv_sem=recv_sems.at[index], device_id=device, device_id_type=mesh_ids,
        )

    def cube_parts(owner, which):
        parts = []
        for chunk in range(chunks):
            at = pl.ds(HALO + which * half + chunk * CHUNK, CHUNK)
            parts.append(copy_to(cube.at[owner, at], cube.at[owner, at], mate))
        return parts

    first_parts = cube_parts(me, partner)
    for chunk, copy in enumerate(first_parts):
        loads[chunk].wait()
        flatten_part(partner * half + chunk * CHUNK, CHUNK)
        if chunk == 0:
            pl.semaphore_wait(barrier, friends)
        copy.start()

    def start_all(copies):
        for goes, _, copy in copies:

            @pl.when(has[goes])
            def _(copy=copy):
                copy.start()

    def arrive_all(copies):
        for _, comes, copy in copies:

            @pl.when(has[comes])
            def _(copy=copy):
                copy.wait_recv()

    def left_all(copies):
        for goes, _, copy in copies:

            @pl.when(has[goes])
            def _(copy=copy):
                copy.wait_send()

    def row_copies(ref, reach):
        top = lambda at: ref.at[pl.ds(at, reach)]
        return [
            ((1, 0), (-1, 0), copy_to(top(HALO + rows - reach), top(HALO - reach), target(1, 0))),
            ((-1, 0), (1, 0), copy_to(top(HALO), top(HALO + rows), target(-1, 0))),
        ]

    def col_copies(out, strips, corners):
        copies = []
        for side, step in ((1, 1), (0, -1)):
            copies.append((
                (0, step), (0, -step),
                copy_to(out.at[side], strips.at[1 - side], target(0, step)),
            ))
            for low, turn in ((0, 1), (1, -1)):
                group = groups - 1 if turn == 1 else 0
                copies.append((
                    (turn, step), (-turn, -step),
                    copy_to(out.at[side, :, group], corners.at[1 - side, low], target(turn, step)),
                ))
        return copies

    lane = lax.broadcasted_iota(jnp.int32, (channels, wide), 1)
    early = lane < 64

    def pack_edges(ref, out, kind):
        def body(group, carried):
            left = right = jnp.zeros((channels, wide), jnp.float32)
            for slot in range(PACK):
                at = HALO + group * PACK + slot
                here = (lane >= slot * 8) & (lane < slot * 8 + 8)
                edge = pltpu.roll(ref[at, :, :wide], slot * 8, 1)
                left = jnp.where(here, edge, left)
                edge = pltpu.roll(ref[at, :, cols - wide :], (slot * 8 + 8) % wide, 1)
                right = jnp.where(here, edge, right)
            out[0, kind, group] = left
            out[1, kind, group] = right
            return carried

        lax.fori_loop(0, groups, body, 0)

    def clear_edges(strips, corners):
        for side, step in ((0, -1), (1, 1)):

            @pl.when(jnp.logical_not(has[(0, step)]))
            def _(side=side):
                strips[side] = jnp.zeros(strips.shape[1:], jnp.float32)

            for low, turn in ((0, -1), (1, 1)):

                @pl.when(jnp.logical_not(has[(turn, step)]))
                def _(side=side, low=low):
                    corners[side, low] = jnp.zeros(corners.shape[2:], jnp.float32)

    def clear_rows(ref, first, last, reach):
        zero = jnp.zeros((reach, channels, cols), jnp.float32)

        @pl.when(jnp.logical_not(has[(-1, 0)]))
        def _():
            ref[pl.ds(first, reach)] = zero

        @pl.when(jnp.logical_not(has[(1, 0)]))
        def _():
            ref[pl.ds(last, reach)] = zero

    loads[chunks].wait()
    flatten_part(me * half, half)
    rows_one = row_copies(own, REACH)
    start_all(rows_one)
    pack_edges(own, strips_out, 0)
    cols_one = col_copies(strips_out, strips_in, corners_in)
    start_all(cols_one)
    clear_rows(own, HALO - REACH, HALO + rows, REACH)
    clear_edges(strips_in, corners_in)
    clear_edges(strips_in_two, corners_in_two)
    for kind, reach in ((0, NEAR), (1, REACH)):
        clear_rows(diffs.at[kind], HALO - reach, HALO + rows, reach)
    gram[...] = jnp.zeros(gram.shape, jnp.float32)

    for side in range(2):
        plain, forward, backward = column_weights(
            place["fcol"] * cols + side * wide, count["fcol"] * cols
        )
        plain, forward, backward = [
            jnp.concatenate([values, values], axis=0).astype(jnp.bfloat16)
            for values in (plain, forward, backward)
        ]
        taps_one[side, :, :wide] = plain
        taps_one[side, :, wide:] = forward
        taps_two[side] = backward

    def doubled(ref, strips, corners, kind, group):
        if group is None:
            line = lambda slot: slot if slot < HALO else slot + rows
            edge = lambda side, slot: (corners[side, 0 if slot < HALO else 1, kind],
                                       (slot + HALO) % PACK)
        else:
            line = lambda slot: HALO + group * PACK + slot
            edge = lambda side, slot: (strips[side, kind, group], slot)
        lefts, rights = [], []
        for slot in range(PACK):
            first, second = ref[line(slot), :, :wide], ref[line(slot), :, wide:]
            before, at = edge(0, slot)
            before = pltpu.roll(before, (wide - 8 - at * 8) % wide, 1)
            after, at = edge(1, slot)
            after = pltpu.roll(after, (wide - at * 8) % wide, 1)
            lefts.append(jnp.concatenate([first, jnp.where(early, second, before)], axis=1))
            rights.append(jnp.concatenate([second, jnp.where(early, after, first)], axis=1))
        return [
            jnp.concatenate(split_two(jnp.concatenate(pieces, axis=0)), axis=1)
            for pieces in (lefts, rights)
        ]

    def store_lines(ref, group, lanes_at, values):
        values = values.reshape(PACK, channels, wide)
        if group is None:
            ref[pl.ds(0, HALO), :, lanes_at] = values[:HALO]
            ref[pl.ds(HALO + rows, HALO), :, lanes_at] = values[HALO:]
        else:
            ref[pl.ds(HALO + group * PACK, PACK), :, lanes_at] = values

    dot = functools.partial(jnp.dot, preferred_element_type=jnp.float32)
    spots = (slice(0, wide), slice(wide, cols))

    def analyse(group):
        for side, values in enumerate(doubled(own, strips_in, corners_in, 0, group)):
            both = dot(values, taps_one[side])
            store_lines(one_cols, group, spots[side], both[:, :wide])
            store_lines(two_cols, group, spots[side], both[:, wide:])

    def each_group(work):
        def body(group, carried):
            work(group)
            return carried

        lax.fori_loop(0, groups, body, 0)
        work(None)

    arrive_all(rows_one)
    arrive_all(cols_one)
    each_group(analyse)

    def smooth_rows(step, carried):
        at = HALO - 4 + step * 8
        middle[pl.ds(at, 8)] = rows_filter(two_cols, at, 8, 1)
        return carried

    lax.fori_loop(0, (rows + 8) // 8, smooth_rows, 0)
    clear_rows(middle, HALO - 4, HALO + rows, 4)

    def collect(step, carried):
        at = pl.multiple_of(step * 8, 8)
        first = rows_filter(one_cols, HALO + at, 8, 1)
        second = rows_filter(middle, HALO + at, 8, 2)
        coarse[0, pl.ds(at, 8)] = first
        coarse[1, pl.ds(at, 8)] = second
        bands = (own[pl.ds(HALO + at, 8)] - first, first - second, second)
        for index, band in enumerate(bands):
            square = band * band
            folded = square[:, :8]
            for start in range(8, channels, 8):
                folded = folded + square[:, start : start + 8]
            sums[index, pl.ds(at, 8)] = jnp.sum(jnp.swapaxes(folded, 0, 1), axis=0)
        return carried

    lax.fori_loop(0, rows // 8, collect, 0)
    share_sums = [copy_to(sums.at[index], other_sums.at[index], mate) for index in range(3)]
    share_sums[0].start()
    share_sums[1].start()

    block = 4

    def gram_step(step, total):
        at = HALO + me * half + step * block
        sides = [
            jnp.concatenate([cube[side, at + row] for row in range(block)], axis=1)
            for side in range(2)
        ]
        both = jnp.concatenate(split_two(jnp.concatenate(sides, axis=0)), axis=0)
        return total + lax.dot_general(
            both, both, (((1,), (1,)), ((), ())), preferred_element_type=jnp.float32
        )

    product = jnp.zeros((2 * order, 2 * order), jnp.float32)
    for chunk, copy in enumerate(first_parts):
        copy.wait_recv()
        product = lax.fori_loop(
            chunk * CHUNK // block, (chunk + 1) * CHUNK // block, gram_step, product
        )
    gram[:, :order] = (
        product[:order, :order] + (product[:order, order:] + product[order:, :order])
    ) + product[order:, order:]
    share_gram = copy_to(gram, other_gram, mate)
    share_gram.start()
    share_sums[2].start()
    second_parts = cube_parts(me, me)
    for copy in second_parts:
        copy.start()

    row = lax.broadcasted_iota(jnp.int32, (8, gram.shape[1]), 0)
    spot = lax.broadcasted_iota(jnp.int32, (channels, gram.shape[1]), 0)
    marks = (row, spot == 1, spot == channels - 1)

    def turns(begin, end, carry):
        size = max(step for step in range(1, TURNS + 1) if (end - begin) % step == 0)

        def body(step, carry):
            for index in range(size):
                at = lax.rem(begin + step * size + index + 1, order - 1)
                carry = rank_round(carry, first_on_top(at, spot.shape), marks)
            return carry

        return lax.fori_loop(0, (end - begin) // size, body, carry)

    share_gram.wait_recv()
    state = rank_start(gram[...] + other_gram[...], marks)
    rounds = JSWEEPS * (order - 1)
    pause = rounds // 6
    state = turns(0, pause, state)
    keep_levels.wait()
    for index in range(3):
        share_sums[index].wait_recv()
        levels = band_levels[index] * level_rows[index]
        totals = sums[index] + other_sums[index]
        factors[index] = levels / jnp.sqrt(jnp.maximum(totals, levels * levels))

    def project(step, carried):
        base = pl.multiple_of(step * 8, 8)
        scales = [factors[index, pl.ds(base, 8)] for index in range(3)]
        for line in range(8):
            at = base + line
            first, second = coarse[0, at], coarse[1, at]
            bands = (own[HALO + at] - first, first - second, second)
            dual = [
                band * jnp.broadcast_to(scale[line : line + 1], band.shape)
                for band, scale in zip(bands, scales)
            ]
            duals[at] = dual[0]
            diffs[0, HALO + at] = dual[1] - dual[0]
            diffs[1, HALO + at] = dual[2] - dual[1]
        return carried

    lax.fori_loop(0, rows // 8, project, 0)
    rows_two = row_copies(diffs.at[1], REACH) + row_copies(diffs.at[0], NEAR)
    start_all(rows_two)
    for kind in range(2):
        pack_edges(diffs.at[kind], strips_out_two, kind)
    cols_two = col_copies(strips_out_two, strips_in_two, corners_in_two)
    start_all(cols_two)
    state = turns(pause, rounds, state)
    mixing[...] = rank_finish(state, threshold)

    arrive_all(rows_two)
    arrive_all(cols_two)

    def synthesise(group):
        edges = (strips_in_two, corners_in_two)
        for side, values in enumerate(doubled(diffs.at[0], *edges, 0, group)):
            store_lines(one_cols, group, spots[side], dot(values, taps_one[side, :, :wide]))
        for side, values in enumerate(doubled(diffs.at[1], *edges, 1, group)):
            store_lines(two_cols, group, spots[side], dot(values, taps_two[side]))

    each_group(synthesise)

    def gather_rows(step, carried):
        at = HALO - NEAR + step * 4
        middle[pl.ds(at, 4)] = one_cols[pl.ds(at, 4)] + rows_filter(two_cols, at, 4, 2)
        return carried

    lax.fori_loop(0, (rows + 2 * NEAR) // 4, gather_rows, 0)
    clear_rows(middle, HALO - NEAR, HALO + rows, NEAR)

    def deliver(step, carried):
        at = pl.multiple_of(step * 8, 8)
        result = duals[pl.ds(at, 8)] + rows_filter(middle, HALO + at, 8, 1)
        back_ref[:, pl.ds(at, 8), :] = jnp.swapaxes(result, 0, 1)
        return carried

    lax.fori_loop(0, rows // 8, deliver, 0)

    own_rows = pl.ds(pl.multiple_of(me * channels, channels), channels)
    high, low = split_two(mixing[own_rows, :order])
    left = jnp.concatenate([high, high, low, low], axis=1)

    def rank_block(at):
        lines = []
        for line in range(8):
            values = jnp.concatenate(
                [cube[0, HALO + at + line], cube[1, HALO + at + line]], axis=0
            )
            high, low = split_two(values)
            lines.append(dot(left, jnp.concatenate([high, low, high, low], axis=0)))
        result = jnp.concatenate([values[None] for values in lines], axis=0)
        rank_ref[:, pl.ds(at, 8), :] = jnp.swapaxes(result, 0, 1)

    def rank_step(step, carried):
        rank_block(pl.multiple_of(me * half + step * 8, 8))
        return carried

    lax.fori_loop(0, half // 8, rank_step, 0)
    for chunk, copy in enumerate(second_parts):
        copy.wait_recv()
        for step in range(CHUNK // 8):
            rank_block(pl.multiple_of(partner * half + chunk * CHUNK + step * 8, 8))
    for copies in (rows_one, cols_one, rows_two, cols_two):
        left_all(copies)
    for copy in (*first_parts, *second_parts, *share_sums, share_gram):
        copy.wait_send()


def output_kernel(back_ref, rank_ref, back_out, rank_out, sems):
    copies = []
    size = back_ref.shape[0] // PIECES
    for source, sink in ((back_ref, back_out), (rank_ref, rank_out)):
        for piece in range(PIECES):
            at = pl.ds(piece * size, size)
            copies.append(pltpu.make_async_copy(
                source.at[at], sink.at[at], sems.at[len(copies)]))
            copies[-1].start()
    for copy in copies:
        copy.wait()


def shards(image_cube, weights):
    channels, rows, cols = image_cube.shape
    threshold = rank_level * math.sqrt(rows * cols)
    order = channels * lax.axis_size("chan")
    tall = rows + 2 * HALO
    groups = rows // PACK
    f32 = jnp.float32
    in_hbm = pl.BlockSpec(memory_space=pltpu.HBM)
    in_vmem = pl.BlockSpec(memory_space=pltpu.VMEM)
    vmem = pltpu.VMEM
    lines = (tall, channels, cols)
    copies = 64
    stay = lambda array: pltpu.with_memory_space_constraint(array, pltpu.HBM)
    held = pl.pallas_call(
        functools.partial(facet_kernel, threshold),
        out_shape=(
            jax.ShapeDtypeStruct(image_cube.shape, f32),
            jax.ShapeDtypeStruct(image_cube.shape, f32),
        ),
        in_specs=[in_hbm, in_hbm],
        out_specs=(in_vmem, in_vmem),
        scratch_shapes=[
            vmem(image_cube.shape, f32),
            vmem((3, rows, cols), f32),
            vmem((2, *lines), f32),
            vmem(lines, f32),
            vmem(lines, f32),
            vmem(lines, f32),
            vmem((2, rows, channels, cols), f32),
            vmem((3, rows, cols), f32),
            vmem((3, rows, cols), f32),
            vmem((3, rows, cols), f32),
            vmem((rows, channels, cols), f32),
            vmem((2, *lines), f32),
            vmem((order, 128), f32),
            vmem((order, 128), f32),
            vmem((128, 128), f32),
            vmem((2, 512, 256), jnp.bfloat16),
            vmem((2, 512, 128), jnp.bfloat16),
            vmem((2, 1, groups, channels, 128), f32),
            vmem((2, 1, groups, channels, 128), f32),
            vmem((2, 2, 1, channels, 128), f32),
            vmem((2, 2, groups, channels, 128), f32),
            vmem((2, 2, groups, channels, 128), f32),
            vmem((2, 2, 2, channels, 128), f32),
            pltpu.SemaphoreType.DMA((copies,)),
            pltpu.SemaphoreType.DMA((copies,)),
            pltpu.SemaphoreType.DMA((rows // 2 // CHUNK + 2,)),
        ],
        compiler_params=pltpu.CompilerParams(
            collective_id=0, has_side_effects=True, vmem_limit_bytes=50 * 2**20
        ),
    )(stay(image_cube), stay(weights))
    return pl.pallas_call(
        output_kernel,
        out_shape=(
            jax.ShapeDtypeStruct(image_cube.shape, f32),
            jax.ShapeDtypeStruct(image_cube.shape, f32),
        ),
        in_specs=[in_vmem, in_vmem],
        out_specs=(in_hbm, in_hbm),
        scratch_shapes=[pltpu.SemaphoreType.DMA((2 * PIECES,))],
        compiler_params=pltpu.CompilerParams(vmem_limit_bytes=4 * 2**20),
    )(*held)


def solution(mesh):
    placed = (P("chan", "frow", "fcol"), P(None, "frow", "fcol"))
    return jax.shard_map(
        shards,
        mesh=mesh,
        in_specs=placed,
        out_specs=(P("chan", "frow", "fcol"), P("chan", "frow", "fcol")),
        check_vma=False,
    )
```

```python
import functools
import math

import jax
import jax.numpy as jnp
from jax import lax
from jax.experimental import pallas as pl
from jax.experimental.pallas import tpu as pltpu
from jax.sharding import PartitionSpec as P

JSWEEPS = 3
HALO = 8
REACH = 6
NEAR = 2
PACK = 16
CHUNK = 8
TURNS = 31
PIECES = 4

filter_taps = (0.0625, 0.25, 0.375, 0.25, 0.0625)
band_levels = (12.0, 4.0, 2.5)
rank_level = 2.0


def down(x, row):
    top, low = x[:8], x[8:]
    a, b = pltpu.roll(top, 1, 0), pltpu.roll(low, 1, 0)
    first = row == 0
    return jnp.concatenate([jnp.where(first, top, a), jnp.where(first, a, b)], axis=0)

def up(x, row):
    top, low = x[:8], x[8:]
    a, b = pltpu.roll(top, 7, 0), pltpu.roll(low, 7, 0)
    final = row == 7
    return jnp.concatenate([jnp.where(final, b, a), jnp.where(final, low, b)], axis=0)

def lanes(x):
    return jnp.broadcast_to(jnp.sum(x, axis=1, keepdims=True), x.shape)

def moved(state, row):
    bt, bl, wt, wl = state
    return [down(v, row) for v in (bt, bl, wt, wl)], [up(v, row) for v in (bt, bl, wt, wl)]

def ahead(moves):
    (bt, bl, _, _), (_, _, wt, wl) = moves
    return lanes(bt * wt), lanes(bt * wl), lanes(bl * wt), lanes(bl * wl)

def rotation(gap, cross, first):
    double = cross + cross
    size = gap * gap + double * double
    flat = size < 1e-36
    inverse = lax.rsqrt(jnp.maximum(size, 1e-36))
    positive = (gap > 0) | ((gap == 0) & first)
    square = jnp.where(flat, 1.0, 0.5 + (0.5 * jnp.abs(gap)) * inverse)
    part = jnp.where(flat, 0.0, jnp.where(positive, cross, -cross) * inverse)
    root = lax.rsqrt(square)
    sine = part * root
    return square * root, sine, sine * root * cross

def rank_round(carry, tie, marks):
    vectors, diag, dots, turn = carry
    row, second, final = marks
    (cosine, sine, shift) = turn
    top, low = diag[0] - shift, diag[1] + shift
    cd, sd, cu, su = down(cosine, row), down(sine, row), up(cosine, row), up(sine, row)
    alpha, beta = jnp.where(second, sd, cd), jnp.where(second, cd, -sd)
    gamma, delta = jnp.where(final, cu, su), jnp.where(final, -su, cu)
    cross = alpha * (gamma * dots[0] + delta * dots[1]) + beta * (gamma * dots[2] + delta * dots[3])
    new_top = jnp.where(second, down(low, row), down(top, row))
    new_low = jnp.where(final, up(top, row), up(low, row))
    turn = rotation(new_low - new_top, cross, tie)
    (dbt, dbl, dwt, dwl), (ubt, ubl, uwt, uwl) = moved(vectors, row)
    vectors = (alpha * dbt + beta * dbl, gamma * ubt + delta * ubl, alpha * dwt + beta * dwl, gamma * uwt + delta * uwl)
    return vectors, (new_top, new_low), ahead(moved(vectors, row)), turn

def first_on_top(index, shape):
    place = lax.broadcasted_iota(jnp.int32, shape, 0)
    cycle = 2 * shape[0] - 1
    top = place - 1 - index
    top = jnp.where(place == 0, -1, jnp.where(top < 0, top + cycle, top))
    low = cycle - 1 - place - index
    low = jnp.where(low < 0, low + cycle, low)
    return top < low


def rank_start(gram, marks):
    row = marks[0]
    half = gram.shape[0] // 2
    shape = (half, gram.shape[1])
    place = lax.broadcasted_iota(jnp.int32, shape, 0)
    lane = lax.broadcasted_iota(jnp.int32, shape, 1)
    low = jnp.zeros(shape, jnp.float32)
    for index in range(half):
        line = gram[2 * half - 1 - index : 2 * half - index]
        low = jnp.where(place == index, jnp.broadcast_to(line, shape), low)
    sides = (jnp.where(lane == place, 1.0, 0.0), jnp.where(lane == 2 * half - 1 - place, 1.0, 0.0))
    vectors = (gram[:half], low, *sides)
    diag = (lanes(gram[:half] * sides[0]), lanes(low * sides[1]))
    turn = rotation(diag[1] - diag[0], lanes(gram[:half] * sides[1]), first_on_top(0, shape))
    return vectors, diag, ahead(moved(vectors, row)), turn


def rank_finish(carry, threshold):
    vectors, diag = carry[0], carry[1]
    sides, values = jnp.concatenate(vectors[2:], axis=0), jnp.concatenate(diag, axis=0)
    factor = 1.0 - threshold / jnp.sqrt(jnp.maximum(values, threshold * threshold))
    return lax.dot_general(
        sides * factor, sides, (((0,), (0,)), ((), ())),
        precision=lax.Precision.HIGHEST, preferred_element_type=jnp.float32,
    )


def split_two(values):
    high = values.astype(jnp.bfloat16)
    low = (values - high.astype(jnp.float32)).astype(jnp.bfloat16)
    return high, low


def tap(offset):
    near = jnp.abs(offset)
    return jnp.where(
        near == 0, filter_taps[2],
        jnp.where(near == 1, filter_taps[3], jnp.where(near == 2, filter_taps[4], 0.0)),
    )


def column_weights(start, total):
    shape = (256, 128)
    source = lax.broadcasted_iota(jnp.int32, shape, 0)
    target = lax.broadcasted_iota(jnp.int32, shape, 1)
    source = jnp.where(source < 192, source, source - 256)
    scale = filter_taps[0]
    one = tap(source - target) * scale
    forward, backward = 0.0, 0.0
    for step in range(-2, 3):
        weight = filter_taps[step + 2] * scale * scale
        between = target + 2 * step
        keep = (between + start >= 0) & (between + start < total)
        forward = forward + jnp.where(keep, weight * tap(source - between), 0.0)
        between = target + step
        keep = (between + start >= 0) & (between + start < total)
        away = source - between
        wide = jnp.where(away % 2 == 0, tap(away // 2), 0.0)
        backward = backward + jnp.where(keep, weight * wide, 0.0)
    return one, forward, backward


def rows_filter(ref, at, count, dilation):
    part = lambda step: ref[pl.ds(at + step * dilation, count)]
    return (part(-2) + part(2)) + 4.0 * (part(-1) + part(1)) + 6.0 * part(0)


def facet_kernel(
    threshold, image_ref, weights_ref, back_ref, rank_ref,
    raw, factors, cube, one_cols, two_cols, middle, coarse, level_rows, sums, other_sums,
    duals, diffs, gram, other_gram, mixing, taps_one, taps_two,
    strips_out, strips_in, corners_in, strips_out_two, strips_in_two, corners_in_two,
    send_sems, recv_sems, local_sems,
):
    channels, rows, cols = image_ref.shape
    wide = cols // 2
    half = rows // 2
    chunks = half // CHUNK
    groups = rows // PACK
    order = 2 * channels
    names = ("frow", "fcol", "chan")
    place = {name: lax.axis_index(name) for name in names}
    count = {name: lax.axis_size(name) for name in names}
    me = place["chan"]
    partner = 1 - me
    mesh_ids = pl.DeviceIdType.MESH
    own = cube.at[me]

    def target(row_step, col_step):
        return (place["frow"] + row_step, place["fcol"] + col_step, me)

    def exists(row_step, col_step):
        found = None
        for name, step in (("frow", row_step), ("fcol", col_step)):
            if step:
                here = place[name] < count[name] - 1 if step > 0 else place[name] > 0
                found = here if found is None else found & here
        return found

    around = [(r, c) for r in (-1, 0, 1) for c in (-1, 0, 1) if (r, c) != (0, 0)]
    has = {key: exists(*key) for key in around}
    mate = (place["frow"], place["fcol"], partner)
    barrier = pltpu.get_barrier_semaphore()
    pl.semaphore_signal(barrier, inc=1, device_id=mate, device_id_type=mesh_ids)
    friends = 1
    for key in around:

        @pl.when(has[key])
        def _(key=key):
            pl.semaphore_signal(barrier, inc=1, device_id=target(*key), device_id_type=mesh_ids)

        friends = friends + jnp.where(has[key], 1, 0)

    loads = []
    for chunk in range(chunks + 1):
        if chunk < chunks:
            at = pl.ds(pl.multiple_of(partner * half + chunk * CHUNK, CHUNK), CHUNK)
        else:
            at = pl.ds(pl.multiple_of(me * half, half), half)
        loads.append(pltpu.make_async_copy(
            image_ref.at[:, at], raw.at[:, at], local_sems.at[chunk]))
        loads[-1].start()
    keep_levels = pltpu.make_async_copy(weights_ref, level_rows, local_sems.at[chunks + 1])
    keep_levels.start()

    def flatten_part(start, size):
        def body(step, carried):
            at = pl.multiple_of(start + step * 8, 8)
            own[pl.ds(HALO + at, 8)] = jnp.swapaxes(raw[:, pl.ds(at, 8), :], 0, 1)
            return carried

        lax.fori_loop(0, size // 8, body, 0)

    used = [0]

    def copy_to(source, sink, device):
        index = used[0]
        used[0] += 1
        return pltpu.make_async_remote_copy(
            src_ref=source, dst_ref=sink, send_sem=send_sems.at[index],
            recv_sem=recv_sems.at[index], device_id=device, device_id_type=mesh_ids,
        )

    def cube_parts(owner, which):
        parts = []
        for chunk in range(chunks):
            at = pl.ds(HALO + which * half + chunk * CHUNK, CHUNK)
            parts.append(copy_to(cube.at[owner, at], cube.at[owner, at], mate))
        return parts

    first_parts = cube_parts(me, partner)
    for chunk, copy in enumerate(first_parts):
        loads[chunk].wait()
        flatten_part(partner * half + chunk * CHUNK, CHUNK)
        if chunk == 0:
            pl.semaphore_wait(barrier, friends)
        copy.start()

    def start_all(copies):
        for goes, _, copy in copies:

            @pl.when(has[goes])
            def _(copy=copy):
                copy.start()

    def arrive_all(copies):
        for _, comes, copy in copies:

            @pl.when(has[comes])
            def _(copy=copy):
                copy.wait_recv()

    def left_all(copies):
        for goes, _, copy in copies:

            @pl.when(has[goes])
            def _(copy=copy):
                copy.wait_send()

    def row_copies(ref, reach):
        top = lambda at: ref.at[pl.ds(at, reach)]
        return [
            ((1, 0), (-1, 0), copy_to(top(HALO + rows - reach), top(HALO - reach), target(1, 0))),
            ((-1, 0), (1, 0), copy_to(top(HALO), top(HALO + rows), target(-1, 0))),
        ]

    def col_copies(out, strips, corners):
        copies = []
        for side, step in ((1, 1), (0, -1)):
            copies.append((
                (0, step), (0, -step),
                copy_to(out.at[side], strips.at[1 - side], target(0, step)),
            ))
            for low, turn in ((0, 1), (1, -1)):
                group = groups - 1 if turn == 1 else 0
                copies.append((
                    (turn, step), (-turn, -step),
                    copy_to(out.at[side, :, group], corners.at[1 - side, low], target(turn, step)),
                ))
        return copies

    lane = lax.broadcasted_iota(jnp.int32, (channels, wide), 1)
    early = lane < 64

    def pack_edges(ref, out, kind):
        def body(group, carried):
            left = right = jnp.zeros((channels, wide), jnp.float32)
            for slot in range(PACK):
                at = HALO + group * PACK + slot
                here = (lane >= slot * 8) & (lane < slot * 8 + 8)
                edge = pltpu.roll(ref[at, :, :wide], slot * 8, 1)
                left = jnp.where(here, edge, left)
                edge = pltpu.roll(ref[at, :, cols - wide :], (slot * 8 + 8) % wide, 1)
                right = jnp.where(here, edge, right)
            out[0, kind, group] = left
            out[1, kind, group] = right
            return carried

        lax.fori_loop(0, groups, body, 0)

    def clear_edges(strips, corners):
        for side, step in ((0, -1), (1, 1)):

            @pl.when(jnp.logical_not(has[(0, step)]))
            def _(side=side):
                strips[side] = jnp.zeros(strips.shape[1:], jnp.float32)

            for low, turn in ((0, -1), (1, 1)):

                @pl.when(jnp.logical_not(has[(turn, step)]))
                def _(side=side, low=low):
                    corners[side, low] = jnp.zeros(corners.shape[2:], jnp.float32)

    def clear_rows(ref, first, last, reach):
        zero = jnp.zeros((reach, channels, cols), jnp.float32)

        @pl.when(jnp.logical_not(has[(-1, 0)]))
        def _():
            ref[pl.ds(first, reach)] = zero

        @pl.when(jnp.logical_not(has[(1, 0)]))
        def _():
            ref[pl.ds(last, reach)] = zero

    loads[chunks].wait()
    flatten_part(me * half, half)
    rows_one = row_copies(own, REACH)
    start_all(rows_one)
    pack_edges(own, strips_out, 0)
    cols_one = col_copies(strips_out, strips_in, corners_in)
    start_all(cols_one)
    clear_rows(own, HALO - REACH, HALO + rows, REACH)
    clear_edges(strips_in, corners_in)
    clear_edges(strips_in_two, corners_in_two)
    for kind, reach in ((0, NEAR), (1, REACH)):
        clear_rows(diffs.at[kind], HALO - reach, HALO + rows, reach)
    gram[...] = jnp.zeros(gram.shape, jnp.float32)

    for side in range(2):
        plain, forward, backward = column_weights(
            place["fcol"] * cols + side * wide, count["fcol"] * cols
        )
        plain, forward, backward = [
            jnp.concatenate([values, values], axis=0).astype(jnp.bfloat16)
            for values in (plain, forward, backward)
        ]
        taps_one[side, :, :wide] = plain
        taps_one[side, :, wide:] = forward
        taps_two[side, :, :wide] = plain
        taps_two[side, :, wide:] = backward

    def doubled(ref, strips, corners, kind, group):
        if group is None:
            line = lambda slot: slot if slot < HALO else slot + rows
            edge = lambda side, slot: (corners[side, 0 if slot < HALO else 1, kind],
                                       (slot + HALO) % PACK)
        else:
            line = lambda slot: HALO + group * PACK + slot
            edge = lambda side, slot: (strips[side, kind, group], slot)
        lefts, rights = [], []
        for slot in range(PACK):
            first, second = ref[line(slot), :, :wide], ref[line(slot), :, wide:]
            before, at = edge(0, slot)
            before = pltpu.roll(before, (wide - 8 - at * 8) % wide, 1)
            after, at = edge(1, slot)
            after = pltpu.roll(after, (wide - at * 8) % wide, 1)
            lefts.append(jnp.concatenate([first, jnp.where(early, second, before)], axis=1))
            rights.append(jnp.concatenate([second, jnp.where(early, after, first)], axis=1))
        return [
            jnp.concatenate(split_two(jnp.concatenate(pieces, axis=0)), axis=1)
            for pieces in (lefts, rights)
        ]

    def store_lines(ref, group, lanes_at, values):
        values = values.reshape(PACK, channels, wide)
        if group is None:
            ref[pl.ds(0, HALO), :, lanes_at] = values[:HALO]
            ref[pl.ds(HALO + rows, HALO), :, lanes_at] = values[HALO:]
        else:
            ref[pl.ds(HALO + group * PACK, PACK), :, lanes_at] = values

    dot = functools.partial(jnp.dot, preferred_element_type=jnp.float32)
    spots = (slice(0, wide), slice(wide, cols))

    def analyse(group):
        for side, values in enumerate(doubled(own, strips_in, corners_in, 0, group)):
            both = dot(values, taps_one[side])
            store_lines(one_cols, group, spots[side], both[:, :wide])
            store_lines(two_cols, group, spots[side], both[:, wide:])

    def each_group(work):
        def body(group, carried):
            work(group)
            return carried

        lax.fori_loop(0, groups, body, 0)
        work(None)

    arrive_all(rows_one)
    arrive_all(cols_one)
    each_group(analyse)

    def smooth_rows(step, carried):
        at = HALO - 4 + step * 8
        middle[pl.ds(at, 8)] = rows_filter(two_cols, at, 8, 1)
        return carried

    lax.fori_loop(0, (rows + 8) // 8, smooth_rows, 0)
    clear_rows(middle, HALO - 4, HALO + rows, 4)

    def collect(step, carried):
        at = pl.multiple_of(step * 8, 8)
        first = rows_filter(one_cols, HALO + at, 8, 1)
        second = rows_filter(middle, HALO + at, 8, 2)
        coarse[0, pl.ds(at, 8)] = first
        coarse[1, pl.ds(at, 8)] = second
        bands = (own[pl.ds(HALO + at, 8)] - first, first - second, second)
        for index, band in enumerate(bands):
            square = band * band
            folded = square[:, :8]
            for start in range(8, channels, 8):
                folded = folded + square[:, start : start + 8]
            sums[index, pl.ds(at, 8)] = jnp.sum(jnp.swapaxes(folded, 0, 1), axis=0)
        return carried

    lax.fori_loop(0, rows // 8, collect, 0)
    share_sums = [copy_to(sums.at[index], other_sums.at[index], mate) for index in range(3)]
    share_sums[0].start()
    share_sums[1].start()

    block = 4

    def gram_step(step, total):
        at = HALO + me * half + step * block
        sides = [
            jnp.concatenate([cube[side, at + row] for row in range(block)], axis=1)
            for side in range(2)
        ]
        both = jnp.concatenate(split_two(jnp.concatenate(sides, axis=0)), axis=0)
        return total + lax.dot_general(
            both, both, (((1,), (1,)), ((), ())), preferred_element_type=jnp.float32
        )

    product = jnp.zeros((2 * order, 2 * order), jnp.float32)
    for chunk, copy in enumerate(first_parts):
        copy.wait_recv()
        product = lax.fori_loop(
            chunk * CHUNK // block, (chunk + 1) * CHUNK // block, gram_step, product
        )
    gram[:, :order] = (
        product[:order, :order] + (product[:order, order:] + product[order:, :order])
    ) + product[order:, order:]
    share_gram = copy_to(gram, other_gram, mate)
    share_gram.start()
    share_sums[2].start()
    second_parts = cube_parts(me, me)
    for copy in second_parts:
        copy.start()

    row = lax.broadcasted_iota(jnp.int32, (8, gram.shape[1]), 0)
    spot = lax.broadcasted_iota(jnp.int32, (channels, gram.shape[1]), 0)
    marks = (row, spot == 1, spot == channels - 1)

    def turns(begin, end, carry):
        size = max(step for step in range(1, TURNS + 1) if (end - begin) % step == 0)

        def body(step, carry):
            for index in range(size):
                at = lax.rem(begin + step * size + index + 1, order - 1)
                carry = rank_round(carry, first_on_top(at, spot.shape), marks)
            return carry

        return lax.fori_loop(0, (end - begin) // size, body, carry)

    share_gram.wait_recv()
    state = rank_start(gram[...] + other_gram[...], marks)
    rounds = JSWEEPS * (order - 1)
    pause = rounds // 6
    state = turns(0, pause, state)
    keep_levels.wait()
    for index in range(3):
        share_sums[index].wait_recv()
        levels = band_levels[index] * level_rows[index]
        totals = sums[index] + other_sums[index]
        factors[index] = levels / jnp.sqrt(jnp.maximum(totals, levels * levels))

    def project(step, carried):
        base = pl.multiple_of(step * 8, 8)
        scales = [factors[index, pl.ds(base, 8)] for index in range(3)]
        for line in range(8):
            at = base + line
            first, second = coarse[0, at], coarse[1, at]
            bands = (own[HALO + at] - first, first - second, second)
            dual = [
                band * jnp.broadcast_to(scale[line : line + 1], band.shape)
                for band, scale in zip(bands, scales)
            ]
            duals[at] = dual[0]
            diffs[0, HALO + at] = dual[1] - dual[0]
            diffs[1, HALO + at] = dual[2] - dual[1]
        return carried

    lax.fori_loop(0, rows // 8, project, 0)
    rows_two = row_copies(diffs.at[1], REACH) + row_copies(diffs.at[0], NEAR)
    start_all(rows_two)
    for kind in range(2):
        pack_edges(diffs.at[kind], strips_out_two, kind)
    cols_two = col_copies(strips_out_two, strips_in_two, corners_in_two)
    start_all(cols_two)
    state = turns(pause, rounds, state)
    mixing[...] = rank_finish(state, threshold)

    arrive_all(rows_two)
    arrive_all(cols_two)

    def synthesise(group):
        edges = (strips_in_two, corners_in_two)
        kinds = [doubled(diffs.at[kind], *edges, kind, group) for kind in range(2)]
        for side, values in enumerate(zip(*kinds)):
            both = dot(jnp.concatenate(values, axis=0), taps_two[side])
            outer, inner = both[: PACK * channels], both[PACK * channels :]
            store_lines(one_cols, group, spots[side], outer[:, :wide])
            store_lines(two_cols, group, spots[side], inner[:, wide:])

    each_group(synthesise)

    def gather_rows(step, carried):
        at = HALO - NEAR + step * 4
        middle[pl.ds(at, 4)] = one_cols[pl.ds(at, 4)] + rows_filter(two_cols, at, 4, 2)
        return carried

    lax.fori_loop(0, (rows + 2 * NEAR) // 4, gather_rows, 0)
    clear_rows(middle, HALO - NEAR, HALO + rows, NEAR)

    def deliver(step, carried):
        at = pl.multiple_of(step * 8, 8)
        result = duals[pl.ds(at, 8)] + rows_filter(middle, HALO + at, 8, 1)
        back_ref[:, pl.ds(at, 8), :] = jnp.swapaxes(result, 0, 1)
        return carried

    lax.fori_loop(0, rows // 8, deliver, 0)

    own_rows = pl.ds(pl.multiple_of(me * channels, channels), channels)
    high, low = split_two(mixing[own_rows, :order])
    left = jnp.concatenate([high, high, low, low], axis=1)

    def rank_block(at):
        lines = []
        for line in range(8):
            values = jnp.concatenate(
                [cube[0, HALO + at + line], cube[1, HALO + at + line]], axis=0
            )
            high, low = split_two(values)
            lines.append(dot(left, jnp.concatenate([high, low, high, low], axis=0)))
        result = jnp.concatenate([values[None] for values in lines], axis=0)
        rank_ref[:, pl.ds(at, 8), :] = jnp.swapaxes(result, 0, 1)

    def rank_step(step, carried):
        rank_block(pl.multiple_of(me * half + step * 8, 8))
        return carried

    lax.fori_loop(0, half // 8, rank_step, 0)
    for chunk, copy in enumerate(second_parts):
        copy.wait_recv()
        for step in range(CHUNK // 8):
            rank_block(pl.multiple_of(partner * half + chunk * CHUNK + step * 8, 8))
    for copies in (rows_one, cols_one, rows_two, cols_two):
        left_all(copies)
    for copy in (*first_parts, *second_parts, *share_sums, share_gram):
        copy.wait_send()


def output_kernel(back_ref, rank_ref, back_out, rank_out, sems):
    copies = []
    size = back_ref.shape[0] // PIECES
    for source, sink in ((back_ref, back_out), (rank_ref, rank_out)):
        for piece in range(PIECES):
            at = pl.ds(piece * size, size)
            copies.append(pltpu.make_async_copy(
                source.at[at], sink.at[at], sems.at[len(copies)]))
            copies[-1].start()
    for copy in copies:
        copy.wait()


def shards(image_cube, weights):
    channels, rows, cols = image_cube.shape
    threshold = rank_level * math.sqrt(rows * cols)
    order = channels * lax.axis_size("chan")
    tall = rows + 2 * HALO
    groups = rows // PACK
    f32 = jnp.float32
    in_hbm = pl.BlockSpec(memory_space=pltpu.HBM)
    in_vmem = pl.BlockSpec(memory_space=pltpu.VMEM)
    vmem = pltpu.VMEM
    lines = (tall, channels, cols)
    copies = 64
    stay = lambda array: pltpu.with_memory_space_constraint(array, pltpu.HBM)
    held = pl.pallas_call(
        functools.partial(facet_kernel, threshold),
        out_shape=(
            jax.ShapeDtypeStruct(image_cube.shape, f32),
            jax.ShapeDtypeStruct(image_cube.shape, f32),
        ),
        in_specs=[in_hbm, in_hbm],
        out_specs=(in_vmem, in_vmem),
        scratch_shapes=[
            vmem(image_cube.shape, f32),
            vmem((3, rows, cols), f32),
            vmem((2, *lines), f32),
            vmem(lines, f32),
            vmem(lines, f32),
            vmem(lines, f32),
            vmem((2, rows, channels, cols), f32),
            vmem((3, rows, cols), f32),
            vmem((3, rows, cols), f32),
            vmem((3, rows, cols), f32),
            vmem((rows, channels, cols), f32),
            vmem((2, *lines), f32),
            vmem((order, 128), f32),
            vmem((order, 128), f32),
            vmem((128, 128), f32),
            vmem((2, 512, 256), jnp.bfloat16),
            vmem((2, 512, 256), jnp.bfloat16),
            vmem((2, 1, groups, channels, 128), f32),
            vmem((2, 1, groups, channels, 128), f32),
            vmem((2, 2, 1, channels, 128), f32),
            vmem((2, 2, groups, channels, 128), f32),
            vmem((2, 2, groups, channels, 128), f32),
            vmem((2, 2, 2, channels, 128), f32),
            pltpu.SemaphoreType.DMA((copies,)),
            pltpu.SemaphoreType.DMA((copies,)),
            pltpu.SemaphoreType.DMA((rows // 2 // CHUNK + 2,)),
        ],
        compiler_params=pltpu.CompilerParams(
            collective_id=0, has_side_effects=True, vmem_limit_bytes=50 * 2**20
        ),
    )(stay(image_cube), stay(weights))
    return pl.pallas_call(
        output_kernel,
        out_shape=(
            jax.ShapeDtypeStruct(image_cube.shape, f32),
            jax.ShapeDtypeStruct(image_cube.shape, f32),
        ),
        in_specs=[in_vmem, in_vmem],
        out_specs=(in_hbm, in_hbm),
        scratch_shapes=[pltpu.SemaphoreType.DMA((2 * PIECES,))],
        compiler_params=pltpu.CompilerParams(vmem_limit_bytes=4 * 2**20),
    )(*held)


def solution(mesh):
    placed = (P("chan", "frow", "fcol"), P(None, "frow", "fcol"))
    return jax.shard_map(
        shards,
        mesh=mesh,
        in_specs=placed,
        out_specs=(P("chan", "frow", "fcol"), P("chan", "frow", "fcol")),
        check_vma=False,
    )
```
